32 devices in a mesh: copies: 2 (over x), expert: 4 (over y, core), tm: 4 (over z).
Axes of the slice: x: 2, y: 2, z: 4, core: 2. Of those that a mesh axis runs over, the one named last changes fastest.
Arguments:
- tokens: bfloat16 [4, 1024, 2048], P('tm', ('copies', 'expert')), parts along dimension 1, may hold values from -6 to 6
- route_ids: int32 [4, 1024, 6], P('tm', ('copies', 'expert')), parts along dimension 1, may hold values from 0 to 15, all different within a row; in each aligned block of 128 rows (0 to 127, 128 to 255, ..., all dimensions but the last counted through in order) at most 72 rows name the same one
- route_probs: float32 [4, 1024, 6], P('tm', ('copies', 'expert')), parts along dimension 1, may hold values from 0.05 to 1
- step_size: float32 [8], P(('copies', 'tm')), parts along dimension 0, may hold values from 0.2 to 0.6
- start_state: float32 [1024, 2048], P(('copies', 'expert')), parts along dimension 0, may hold values from -6 to 6
- w_gate: bfloat16 [16, 2048, 768], P('expert'), may hold values from -0.125 to 0.125
- w_up: bfloat16 [16, 2048, 768], P('expert'), may hold values from -0.125 to 0.125
- w_down: bfloat16 [16, 768, 2048], P('expert'), may hold values from -0.21875 to 0.21875
Outputs:
- new_iterate: float32 [4, 1024, 2048], P('tm', ('copies', 'expert')), parts along dimension 1
The draws below stay inside these ranges and needn't reach their ends.
There are 2 independent parts, one for each index of `copies`. The reference program is written for one: setup_inputs(seed, part) draws one part's arguments, and reference() takes and returns one part's arrays. A program takes and returns all parts, laid end to end along the dimension named above; an argument that names none is the same for every part. Nothing has to cross between parts.
Inputs may be any that keep to these rules, and one draw needn't show every extreme that they name: `route_ids`: each row names 6 different experts. In each aligned block of 128 rows (the tokens of one device), no expert is named by more than 72 rows, a bound that some block reaches.
All inputs are finite; a program needn't handle non-finite values.
Results may differ from the reference program's by a relative error of at most 0.0018.
Values may be sent and summed in bfloat16 or wider, within the bound.
A program may use at most 128 MiB of HBM per device.

```python
import math
import jax
import jax.numpy as jnp
import numpy as np
from jax import lax

D = 2048
FF = 768
TOPK = 6
TOK_DEV = 128
EXPERTS = 16
C = 72
TIMESTEPS = 4
GROUP_TOK = 512
N_EXPERT = 4


def levels(rng, extent, pieces, smallest, largest):
    def one(dim, parts):
        draws = jax.random.uniform(jax.random.fold_in(jax.random.fold_in(rng, 6), dim), (parts,), jnp.float32, smallest / len(pieces), largest / len(pieces))
        return jnp.repeat(jnp.exp(draws), extent[dim] // parts).reshape((-1,) + (1,) * (len(extent) - dim - 1))

    factor_of = one(*pieces[0])
    for cut in pieces[1:]:
        factor_of = factor_of * one(*cut)
    return factor_of


def assign_block(rng, own, number, rows, count, top, reach, skew):
    order = jax.random.permutation(rng, count)
    packed, ordinary = load_shares(count, rows * top, reach, skew, True), load_shares(count, rows * top, reach, skew, False)
    places = jnp.arange(count)

    def named(lengths, rotation):
        used = int((lengths > 0).sum())
        fixed = max(1, used // 4)
        shifted = fixed + (places - fixed + rotation * (used - fixed)) % max(1, count - fixed)
        return jnp.zeros((count,), jnp.int32).at[order[jnp.where(places < fixed, places, shifted)]].set(jnp.asarray(lengths, jnp.int32))

    lengths = jnp.where(number % 4 == 0, named(packed, number // 4), named(ordinary, number - number // 4 - 1))
    mixed = jax.random.permutation(jax.random.fold_in(own, 3), count)
    donor, receiver = mixed[0:count // 2 * 2:2], mixed[1:count // 2 * 2:2]
    margin = jnp.minimum(lengths[donor] - 1, reach - lengths[receiver]) // 2
    margin = jnp.where((donor == order[0]) | (receiver == order[0]) | (lengths[receiver] == 0), 0, jnp.maximum(margin, 0))
    shifted = jax.random.randint(jax.random.fold_in(own, 4), (count // 2,), 0, 1 << 20) % (margin + 1)
    lengths = lengths.at[donor].add(-shifted).at[receiver].add(shifted)
    labels = jnp.searchsorted(jnp.cumsum(lengths), jnp.arange(rows * top), side="right").astype(jnp.int32)
    listing = labels.reshape(top, rows).T
    listing = listing[jax.random.permutation(jax.random.fold_in(own, 1), rows)]
    rotation = jax.random.randint(jax.random.fold_in(own, 2), (rows, 1), 0, top)
    return jnp.take_along_axis(listing, (jnp.arange(top)[None, :] + rotation) % top, axis=1)


def load_shares(amount, total, reach, slope, full):
    portions = [(1 << 20) // math.isqrt(rank ** slope) + 1 for rank in range(1, amount + 1)]
    largest = reach if full else min(reach, max(-(-total // amount), total * portions[0] // sum(portions)))
    least = 1 if total - largest >= amount - 1 else 0
    counts, spare = [largest] + [least] * (amount - 1), total - largest - least * (amount - 1)
    while spare > 0:
        movable = [i for i in range(1, amount) if counts[i] < largest] or [i for i in range(1, amount) if counts[i] < reach]
        whole, budget = sum([portions[i] for i in movable]), spare
        for i in movable:
            addition = min(reach - counts[i], max(1, budget * portions[i] // whole), spare)
            counts[i] = counts[i] + addition
            spare = spare - addition
    return np.array(counts)


def bell_draw(own_key, extent, spread, bound, split=(), kind=jnp.bfloat16):
    drawn = spread * jax.random.normal(own_key, extent, jnp.float32)
    if split:
        drawn = drawn * levels(own_key, extent, split, -0.22, 0.18)
    return jnp.clip(drawn, -bound, bound).astype(kind)


def setup_inputs(seed: int = 0, part: int = 0) -> dict:
    keys = jax.random.split(jax.random.key(seed), 9)
    part_keys = jax.random.split(jax.random.fold_in(keys[8], part), 9)
    tokens = bell_draw(part_keys[0], (TIMESTEPS, GROUP_TOK, D), 1.0, 6.0, ((0, 4), (1, 4)))
    route_ids_keys = jax.random.split(jax.random.fold_in(part_keys[1], 1), TIMESTEPS * GROUP_TOK // TOK_DEV)
    route_ids_turns = jax.random.permutation(jax.random.fold_in(part_keys[1], 3), TIMESTEPS * GROUP_TOK // TOK_DEV)
    route_ids = jax.vmap(lambda own, number: assign_block(jax.random.fold_in(part_keys[1], 2), own, number, TOK_DEV, EXPERTS, TOPK, C, 2))(route_ids_keys, route_ids_turns).reshape((TIMESTEPS, GROUP_TOK, TOPK))
    route_probs = jnp.clip(0.05 + 0.95 * jax.random.uniform(part_keys[2], (TIMESTEPS, GROUP_TOK, TOPK), jnp.float32) ** levels(part_keys[2], (TIMESTEPS, GROUP_TOK, TOPK), ((0, 4), (1, 4)), -0.2, 0.2), 0.05, 1.0)
    step_size = jnp.clip(jnp.exp(math.log(0.6) - 1.0986123 * jax.random.uniform(part_keys[3], (TIMESTEPS,), jnp.float32) ** levels(part_keys[3], (TIMESTEPS,), ((0, 4),), -0.2, 0.2)), 0.2, 0.6)
    start_state = bell_draw(part_keys[4], (GROUP_TOK, D), 1.0, 6.0, ((0, 4),), jnp.float32)
    w_gate = bell_draw(keys[5], (EXPERTS, D, FF), D ** -0.5, 0.125, ((0, 4),))
    w_up = bell_draw(keys[6], (EXPERTS, D, FF), D ** -0.5, 0.125, ((0, 4),))
    w_down = bell_draw(keys[7], (EXPERTS, FF, D), FF ** -0.5, 0.21875, ((0, 4),))
    return {"tokens": tokens, "route_ids": route_ids, "route_probs": route_probs, "step_size": step_size, "start_state": start_state, "w_gate": w_gate, "w_up": w_up, "w_down": w_down}


def reference(tokens, route_ids, route_probs, step_size, start_state, w_gate, w_up, w_down):
    blocks = TIMESTEPS * N_EXPERT
    values = tokens.astype(jnp.float32)
    normed = (values * lax.rsqrt(lax.optimization_barrier(jnp.mean(values * values, axis=-1, keepdims=True)) + 1e-06)).astype(jnp.bfloat16)
    normed = normed.reshape(blocks, TOK_DEV, D)
    padded = jnp.concatenate([normed, jnp.zeros((blocks, 1, D), jnp.bfloat16)], axis=1)
    flat_ids = route_ids.reshape(blocks, TOK_DEV * TOPK).astype(jnp.int32)
    one_hot = (flat_ids[:, :, None] == jnp.arange(EXPERTS, dtype=jnp.int32)[None, None, :]).astype(jnp.int32)
    earlier = jnp.cumsum(one_hot, axis=1) - one_hot
    position = lax.optimization_barrier(jnp.sum(earlier * one_hot, axis=2)).astype(jnp.int32)
    slot_index = (flat_ids * C + position).astype(jnp.int32)
    gate_probs = route_probs.astype(jnp.float32)
    weights = (gate_probs / lax.optimization_barrier(jnp.sum(gate_probs, axis=-1, keepdims=True))).reshape(blocks, TOK_DEV * TOPK)
    block_ids = jnp.arange(blocks, dtype=jnp.int32)[:, None]
    token_of = jnp.broadcast_to((jnp.arange(TOK_DEV * TOPK, dtype=jnp.int32) // TOPK)[None, :], slot_index.shape)
    slot_table = jnp.full((blocks, EXPERTS * C), TOK_DEV, jnp.int32).at[block_ids, slot_index].set(token_of)
    weight_table = jnp.zeros((blocks, EXPERTS * C), jnp.float32).at[block_ids, slot_index].set(weights)

    def expert_step(drift_rows, operands):
        gate_one, up_one, down_one, expert = operands
        slot_tokens = lax.dynamic_slice_in_dim(slot_table, expert * C, C, 1)
        scales = lax.dynamic_slice_in_dim(weight_table, expert * C, C, 1)
        slot_rows = jnp.take_along_axis(padded, slot_tokens[:, :, None], axis=1).reshape(blocks * C, D)
        gate_act = jnp.dot(slot_rows, gate_one, preferred_element_type=jnp.float32)
        up_act = jnp.dot(slot_rows, up_one, preferred_element_type=jnp.float32)
        hidden = (jax.nn.silu(gate_act) * up_act).astype(jnp.bfloat16)
        result = jnp.dot(hidden, down_one, preferred_element_type=jnp.float32).astype(jnp.bfloat16)
        result = lax.optimization_barrier(result).astype(jnp.float32).reshape(blocks, C, D)
        drift_rows = drift_rows.at[block_ids, slot_tokens].add(scales[:, :, None] * result)
        return (drift_rows, None)
    initial = jnp.zeros((blocks, TOK_DEV + 1, D), jnp.float32)
    drift_rows, unused_out = lax.scan(expert_step, initial, (w_gate, w_up, w_down, jnp.arange(EXPERTS, dtype=jnp.int32)))
    drift_rows = drift_rows[:, :TOK_DEV, :].reshape(TIMESTEPS, GROUP_TOK, D)
    increment = step_size.astype(jnp.float32)[:, None, None] * drift_rows
    return start_state[None, :, :] + jnp.cumsum(increment, axis=0)
```

```python
import functools

import jax
import jax.numpy as jnp
from jax import lax
from jax.experimental import pallas as pl
from jax.experimental.pallas import tpu as pltpu
from jax.sharding import PartitionSpec as P

MESH = pl.DeviceIdType.MESH
BF16 = jnp.bfloat16
F32 = jnp.float32
PARTS = 4
DC = 256
LAG = 3


def fit(total, wanted):
    return wanted if total % wanted == 0 else total


def kernel(
    dims,
    tok_hbm, ids_hbm, probs_hbm, step_in, wg_hbm, wu_hbm, wd_hbm, out_ref,
    wg, wu, wd, raw, tok, ids, probs, scale, rows_own, rows_far, acc_g, acc_u, hid, mmap, ycat,
    keep, px_out, px_in, y_out, y_in, z_out, z_in,
    in_sem, up_sem, down_sem, t_send, f_send, t_recv, i_send, i_recv, p_send, p_recv,
    px_send, px_recv, y_send, y_recv, z_send, z_recv, z_ready,
):
    chips, steps, cap, slots, cuts, dc = dims
    local, width, ff = wg.shape
    toks = raw.shape[0]
    topk = ids.shape[2]
    parts = len(cuts) - 1
    chunks = width // dc
    me = lax.axis_index("expert")
    now = lax.axis_index("tm")
    core = lax.rem(me, 2)
    chip = lax.div(me, 2)

    def peer(offset, other):
        own = (1 - core) if other else core
        return {"expert": lax.rem(chip + offset, chips) * 2 + own}

    def remote(src, dst, send, recv, where):
        return pltpu.make_async_remote_copy(
            src_ref=src, dst_ref=dst, send_sem=send, recv_sem=recv,
            device_id=where, device_id_type=MESH,
        )

    def up_copy(kind, e):
        src, dst = ((wg_hbm, wg), (wu_hbm, wu))[kind]
        return pltpu.make_async_copy(src.at[e], dst.at[e], up_sem.at[kind, e])

    def down_copy(e):
        return pltpu.make_async_copy(wd_hbm.at[e], wd.at[e], down_sem.at[e])

    load_tok = pltpu.make_async_copy(tok_hbm, raw, in_sem.at[0])
    load_ids = pltpu.make_async_copy(ids_hbm, ids.at[0, 0], in_sem.at[1])
    load_probs = pltpu.make_async_copy(probs_hbm, probs.at[0, 0], in_sem.at[2])
    load_tok.start()
    load_ids.start()
    load_probs.start()
    for e in range(local):
        for kind in range(2):
            up_copy(kind, e).start()
    for e in range(local):
        down_copy(e).start()

    barrier = pltpu.get_barrier_semaphore()
    for d in range(chips):
        for other in (False, True):
            if d or other:
                pl.semaphore_signal(barrier, inc=1, device_id=peer(d, other), device_id_type=MESH)

    @pl.when(now < steps - 1)
    def _():
        pl.semaphore_signal(barrier, inc=1, device_id={"tm": now + 1}, device_id_type=MESH)

    load_tok.wait()

    def norm(i, carry):
        span = pl.ds(pl.multiple_of(i * 16, 16), 16)
        values = raw[span, :].astype(F32)
        root = lax.rsqrt(jnp.sum(values * values, axis=1, keepdims=True) * (1.0 / width) + 1e-06)
        tok[0, span, :] = (values * root).astype(BF16)
        return carry

    lax.fori_loop(0, toks // 16, norm, 0)
    load_ids.wait()
    load_probs.wait()
    pl.semaphore_wait(barrier, 2 * chips - 1 + jnp.where(now > 0, 1, 0))

    @pl.when(now > 0)
    def _():
        pl.semaphore_signal(z_ready, inc=1, device_id={"tm": now - 1}, device_id_type=MESH)

    def cols_of(q):
        return pl.ds(cuts[q], cuts[q + 1] - cuts[q])

    def tok_copy(d, q):
        slot, side = ((chips - d) % chips, 0) if d else (0, 1)
        return remote(
            tok.at[0, pl.ds(0, toks), cols_of(q)],
            tok.at[slot, pl.ds(side * toks, toks), cols_of(q)],
            t_send.at[d, q], t_recv.at[slot, side, q], peer(d, d == 0),
        )

    def route_copies(d, other):
        slot, side = (chips - d) % chips, int(other)
        where = peer(d, other)
        return (
            remote(
                ids.at[0, 0], ids.at[slot, side], i_send.at[d, side], i_recv.at[slot, side], where
            ),
            remote(
                probs.at[0, 0], probs.at[slot, side],
                p_send.at[d, side], p_recv.at[slot, side], where,
            ),
        )

    def forward_copy(j, q):
        return remote(
            tok.at[j, pl.ds(0, toks), cols_of(q)], tok.at[j, pl.ds(toks, toks), cols_of(q)],
            f_send.at[j, q], t_recv.at[j, 1, q], peer(0, True),
        )

    def tok_arrival(j, side, q):
        span = tok.at[j, pl.ds(side * toks, toks), cols_of(q)]
        return remote(span, span, f_send.at[j, q], t_recv.at[j, side, q], peer(0, True))

    def route_arrivals(j, side):
        where = peer(0, True)
        return (
            remote(ids.at[0, 0], ids.at[j, side], i_send.at[0, 1], i_recv.at[j, side], where),
            remote(probs.at[0, 0], probs.at[j, side], p_send.at[0, 1], p_recv.at[j, side], where),
        )

    for d in range(chips):
        for other in (False, True):
            if d or other:
                for copy in route_copies(d, other):
                    copy.start()
    for q in range(parts):
        for d in range(1, chips):
            tok_copy(d, q).start()
        tok_copy(0, q).start()

    local8 = -(-local // 8) * 8
    earlier = jnp.where(
        lax.broadcasted_iota(jnp.int32, (toks, toks), 0)
        < lax.broadcasted_iota(jnp.int32, (toks, toks), 1),
        1.0, 0.0,
    ).astype(BF16)
    rid = lax.broadcasted_iota(jnp.int32, (slots, toks), 0).astype(F32)
    names = me * local + lax.broadcasted_iota(jnp.int32, (local8, toks), 0)
    step_now = step_in[0]

    def place(id_ref, prob_ref):
        member = jnp.zeros((local8, toks), F32)
        weight = jnp.zeros((local8, toks), F32)
        total = jnp.zeros((1, toks), F32)
        for k in range(topk):
            hit = id_ref[k] == names
            member = member + jnp.where(hit, 1.0, 0.0)
            weight = weight + jnp.where(hit, prob_ref[k], 0.0)
            total = total + prob_ref[k]
        count = jnp.dot(member.astype(BF16), earlier, preferred_element_type=F32)
        return jnp.where(member > 0.0, count, -4096.0), weight * (step_now / total)

    def tables(j, carry):
        near = place(ids.at[j, 0], probs.at[j, 0])
        far = place(ids.at[j, 1], probs.at[j, 1])
        for e in range(local):
            low = rid == near[0][e : e + 1, :]
            high = (rid - cap) == far[0][e : e + 1, :]
            mmap[j, e * slots : (e + 1) * slots, :] = jnp.concatenate(
                [jnp.where(low, 1.0, 0.0), jnp.where(high, 1.0, 0.0)], axis=1
            ).astype(BF16)
            amount = jnp.sum(
                jnp.where(low, near[1][e : e + 1, :], 0.0)
                + jnp.where(high, far[1][e : e + 1, :], 0.0),
                axis=1, keepdims=True,
            )
            scale[j, e] = jnp.broadcast_to(amount, (slots, 128))
        return carry

    for copy in route_arrivals(0, 1):
        copy.wait_recv()
    tables(0, 0)

    def far_tables(j, carry):
        for side in range(2):
            for copy in route_arrivals(j, side):
                copy.wait_recv()
        return tables(j, carry)

    lax.fori_loop(1, chips, far_tables, 0)

    def pass_on(q):
        for j in range(1, chips):
            tok_arrival(j, 0, q).wait_recv()
            forward_copy(j, q).start()

    def loop(first, last, body):
        if last - first == 1:
            body(first, 0)
        else:
            lax.fori_loop(first, last, body, 0)

    def silu_mul(gate, up, amount):
        return (gate / (1.0 + jnp.exp(-gate)) * (up * amount)).astype(BF16)

    def own_rows(e):
        for kind in range(2):
            up_copy(kind, e).wait()
        rows_own[...] = jnp.dot(
            mmap[0, e * slots : (e + 1) * slots, :], tok[0], preferred_element_type=F32
        ).astype(BF16)
        gate = jnp.dot(rows_own[...], wg[e], preferred_element_type=F32)
        up = jnp.dot(rows_own[...], wu[e], preferred_element_type=F32)
        hid[0, e] = silu_mul(gate, up, scale[0, e, :, 0:1])

    def far_rows(q):
        for j in range(1, chips):
            tok_arrival(j, 1, q).wait_recv()
        lo, hi = cuts[q], cuts[q + 1]

        def one(j, carry):
            rows_far[:, 0 : hi - lo] = jnp.dot(
                mmap[j], tok[j, :, lo:hi], preferred_element_type=F32
            ).astype(BF16)
            for e in range(local):
                piece = rows_far[e * slots : (e + 1) * slots, 0 : hi - lo]
                gate = jnp.dot(piece, wg[e, lo:hi, :], preferred_element_type=F32)
                up = jnp.dot(piece, wu[e, lo:hi, :], preferred_element_type=F32)
                if q:
                    gate = gate + acc_g[j - 1, e]
                    up = up + acc_u[j - 1, e]
                if q < parts - 1:
                    acc_g[j - 1, e] = gate
                    acc_u[j - 1, e] = up
                else:
                    hid[j, e] = silu_mul(gate, up, scale[j, e, :, 0:1])
            return carry

        loop(1, chips, one)

    for copy in [tok_arrival(0, 1, q) for q in range(parts)]:
        copy.wait_recv()
    tasks = [functools.partial(own_rows, e) for e in range(local)]
    tasks += [functools.partial(far_rows, q) for q in range(parts)]
    passed = 0
    for i, task in enumerate(tasks):
        while passed < parts and (
            i - local >= passed or (i < local and (i + 1) * parts >= (passed + 1) * (local + 2))
            or (i >= local and passed <= i - local + 1)
        ):
            pass_on(passed)
            passed += 1
        task()

    for e in range(local):
        down_copy(e).wait()

    def pair_copy(j, k):
        return remote(
            px_out.at[j, k], px_in.at[j, k], px_send.at[j, k], px_recv.at[j, k], peer(0, True)
        )

    def back_copy(j, k):
        slot = chips - j
        return remote(
            y_out.at[j, k], y_in.at[slot, k], y_send.at[j, k], y_recv.at[slot, k], peer(j, False)
        )

    def rise_copy(k):
        return remote(
            z_out.at[k], z_in.at[k], z_send.at[k], z_recv.at[k], {"tm": lax.rem(now + 1, steps)}
        )

    def down(k, first, last):
        cols = pl.ds(pl.multiple_of(k * dc, 128), dc)

        def one(j, carry):
            for e in range(local):
                ycat[e * slots : (e + 1) * slots, :] = jnp.dot(
                    hid[j, e], wd[e, :, cols], preferred_element_type=F32
                ).astype(BF16)
            share = lax.dot_general(
                mmap[j], ycat[...], (((0,), (0,)), ((), ())), preferred_element_type=F32
            )
            px_out[j, k] = share[toks:].astype(BF16)
            keep[j, k] = share[:toks]
            pair_copy(j, k).start()
            return carry

        loop(first, last, one)

    def send_back(k):
        for j in range(1, chips):
            pair_copy(j, k).wait_recv()
            y_out[j, k] = (keep[j, k] + px_in[j, k].astype(F32)).astype(BF16)
            back_copy(j, k).start()

    def finish(k):
        cols = pl.ds(pl.multiple_of(k * dc, 128), dc)
        pair_copy(0, k).wait_recv()
        total = keep[0, k] + px_in[0, k].astype(F32)
        for j in range(1, chips):
            back_copy(chips - j, k).wait_recv()
            total = total + y_in[j, k].astype(F32)
        keep[0, k] = total

        @pl.when(now > 0)
        def _():
            rise_copy(k).wait_recv()
            keep[0, k] = keep[0, k] + z_in[k].astype(F32)

        @pl.when(now < steps - 1)
        def _():
            z_out[k] = keep[0, k].astype(BF16)
            rise_copy(k).start()

        out_ref[:, cols] = keep[0, k]

    @pl.when(now < steps - 1)
    def _():
        pl.semaphore_wait(z_ready, 1)

    lag = jnp.minimum(LAG * (now + 1), chunks)

    def step(k, carry):
        down(k, 1, chips)
        down(k, 0, 1)
        send_back(k)

        @pl.when(k >= lag)
        def _():
            finish(k - lag)

        return carry

    lax.fori_loop(0, chunks, step, 0)

    def rest(k, carry):
        finish(k)
        return carry

    lax.fori_loop(chunks - lag, chunks, rest, 0)

    for d in range(chips):
        for other in (False, True):
            if d or other:
                for copy in route_copies(d, other):
                    copy.wait_send()
        for q in range(parts):
            tok_copy(d, q).wait_send()
            if d:
                forward_copy(d, q).wait_send()

    def drain(k, carry):
        for j in range(chips):
            pair_copy(j, k).wait_send()
            if j:
                back_copy(j, k).wait_send()

        @pl.when(now < steps - 1)
        def _():
            rise_copy(k).wait_send()

        return carry

    lax.fori_loop(0, chunks, drain, 0)


def shards(mesh, tokens, route_ids, route_probs, step_size, start_state, w_gate, w_up, w_down):
    toks, width = tokens.shape[1:]
    topk = route_ids.shape[2]
    local, _, ff = w_gate.shape
    group = mesh.shape["expert"]
    steps = mesh.shape["tm"]
    chips = group // 2
    cap = 3 * toks * topk // (2 * local * group)
    slots = -(-2 * cap // 16) * 16
    dc = fit(width, DC)
    chunks = width // dc
    cuts = tuple(width * q // PARTS for q in range(PARTS + 1))
    wide = max(b - a for a, b in zip(cuts, cuts[1:]))

    vmem = pl.BlockSpec(memory_space=pltpu.VMEM)
    smem = pl.BlockSpec(memory_space=pltpu.SMEM)
    hbm = pl.BlockSpec(memory_space=pl.ANY)
    dma = pltpu.SemaphoreType.DMA
    total = pl.pallas_call(
        functools.partial(kernel, (chips, steps, cap, slots, cuts, dc)),
        out_shape=jax.ShapeDtypeStruct((toks, width), F32),
        in_specs=[hbm, hbm, hbm, smem, hbm, hbm, hbm],
        out_specs=vmem,
        scratch_shapes=[
            pltpu.VMEM((local, width, ff), BF16),
            pltpu.VMEM((local, width, ff), BF16),
            pltpu.VMEM((local, ff, width), BF16),
            pltpu.VMEM((toks, width), BF16),
            pltpu.VMEM((chips, 2 * toks, width), BF16),
            pltpu.VMEM((chips, 2, topk, 1, toks), jnp.int32),
            pltpu.VMEM((chips, 2, topk, 1, toks), F32),
            pltpu.VMEM((chips, local, slots, 128), F32),
            pltpu.VMEM((slots, width), BF16),
            pltpu.VMEM((local * slots, wide), BF16),
            pltpu.VMEM((chips - 1, local, slots, ff), F32),
            pltpu.VMEM((chips - 1, local, slots, ff), F32),
            pltpu.VMEM((chips, local, slots, ff), BF16),
            pltpu.VMEM((chips, local * slots, 2 * toks), BF16),
            pltpu.VMEM((local * slots, dc), BF16),
            pltpu.VMEM((chips, chunks, toks, dc), F32),
            pltpu.VMEM((chips, chunks, toks, dc), BF16),
            pltpu.VMEM((chips, chunks, toks, dc), BF16),
            pltpu.VMEM((chips, chunks, toks, dc), BF16),
            pltpu.VMEM((chips, chunks, toks, dc), BF16),
            pltpu.VMEM((chunks, toks, dc), BF16),
            pltpu.VMEM((chunks, toks, dc), BF16),
            dma((3,)),
            dma((2, local)),
            dma((local,)),
            dma((chips, PARTS)),
            dma((chips, PARTS)),
            dma((chips, 2, PARTS)),
            dma((chips, 2)),
            dma((chips, 2)),
            dma((chips, 2)),
            dma((chips, 2)),
            dma((chips, chunks)),
            dma((chips, chunks)),
            dma((chips, chunks)),
            dma((chips, chunks)),
            dma((chunks,)),
            dma((chunks,)),
            pltpu.SemaphoreType.REGULAR,
        ],
        compiler_params=pltpu.CompilerParams(
            collective_id=0, has_side_effects=True, vmem_limit_bytes=67_043_328
        ),
    )(
        tokens[0], jnp.transpose(route_ids, (2, 0, 1)), jnp.transpose(route_probs, (2, 0, 1)),
        step_size, w_gate, w_up, w_down,
    )
    return (start_state + total)[None]


def solution(mesh):
    return jax.shard_map(
        functools.partial(shards, mesh),
        mesh=mesh,
        in_specs=(
            P("tm", ("copies", "expert"), None),
            P("tm", ("copies", "expert"), None),
            P("tm", ("copies", "expert"), None),
            P(("copies", "tm")),
            P(("copies", "expert"), None),
            P("expert", None, None),
            P("expert", None, None),
            P("expert", None, None),
        ),
        out_specs=P("tm", ("copies", "expert"), None),
        check_vma=False,
    )
```

```python
import functools

import jax
import jax.numpy as jnp
from jax import lax
from jax.experimental import pallas as pl
from jax.experimental.pallas import tpu as pltpu
from jax.sharding import PartitionSpec as P

MESH = pl.DeviceIdType.MESH
BF16 = jnp.bfloat16
F32 = jnp.float32
PARTS = 4
DC = 256
LAG = 3


def fit(total, wanted):
    return wanted if total % wanted == 0 else total


def kernel(
    dims,
    tok_hbm, ids_hbm, probs_hbm, step_in, start_hbm, wg_hbm, wu_hbm, wd_hbm, out_ref,
    wg, wu, wd, raw, tok, ids, probs, start, amount, rows_own, rows_far, acc_g, acc_u, hid,
    mmap, ycat,
    keep, px_out, px_in, y_out, y_in, z_out, z_in,
    in_sem, up_sem, down_sem, t_send, f_send, t_recv, w_send, w_recv, i_send, i_recv,
    p_send, p_recv, px_send, px_recv, y_send, y_recv, z_send, z_recv, z_ready,
):
    chips, steps, cap, slots, cuts, dc = dims
    local, width, ff = wg.shape
    toks = start.shape[0]
    topk = ids.shape[2]
    parts = len(cuts) - 1
    chunks = width // dc
    me = lax.axis_index("expert")
    now = lax.axis_index("tm")
    core = lax.rem(me, 2)
    chip = lax.div(me, 2)

    def peer(offset, other):
        own = (1 - core) if other else core
        return {"expert": lax.rem(chip + offset, chips) * 2 + own}

    def remote(src, dst, send, recv, where):
        return pltpu.make_async_remote_copy(
            src_ref=src, dst_ref=dst, send_sem=send, recv_sem=recv,
            device_id=where, device_id_type=MESH,
        )

    def up_copy(kind, e):
        src, dst = ((wg_hbm, wg), (wu_hbm, wu))[kind]
        return pltpu.make_async_copy(src.at[e], dst.at[e], up_sem.at[kind, e])

    def down_copy(e):
        return pltpu.make_async_copy(wd_hbm.at[e], wd.at[e], down_sem.at[e])

    load_tok = pltpu.make_async_copy(tok_hbm, raw, in_sem.at[0])
    load_ids = pltpu.make_async_copy(ids_hbm, ids.at[0, 0], in_sem.at[1])
    load_probs = pltpu.make_async_copy(probs_hbm, probs.at[0, 0], in_sem.at[2])
    load_start = pltpu.make_async_copy(start_hbm, start, in_sem.at[3])

    barrier = pltpu.get_barrier_semaphore()
    for d in range(chips):
        for other in (False, True):
            if d or other:
                pl.semaphore_signal(barrier, inc=1, device_id=peer(d, other), device_id_type=MESH)

    @pl.when(now < steps - 1)
    def _():
        pl.semaphore_signal(barrier, inc=1, device_id={"tm": now + 1}, device_id_type=MESH)

    load_tok.start()
    load_ids.start()
    load_probs.start()
    load_tok.wait()

    def norm(i, carry):
        span = pl.ds(pl.multiple_of(i * 16, 16), 16)
        values = raw[span, :].astype(F32)
        root = lax.rsqrt(jnp.sum(values * values, axis=1, keepdims=True) * (1.0 / width) + 1e-06)
        tok[0, span, :] = (values * root).astype(BF16)
        return carry

    lax.fori_loop(0, toks // 16, norm, 0, unroll=2)
    pl.semaphore_wait(barrier, 2 * chips - 1 + jnp.where(now > 0, 1, 0))

    def cols_of(q):
        return pl.ds(cuts[q], cuts[q + 1] - cuts[q])

    def tok_copy(d, q):
        slot = (chips - d) % chips
        return remote(
            tok.at[0, pl.ds(0, toks), cols_of(q)], tok.at[slot, pl.ds(0, toks), cols_of(q)],
            t_send.at[d, q], t_recv.at[slot, 0, q], peer(d, False),
        )

    twin_copy = remote(
        tok.at[0, pl.ds(0, toks)], tok.at[0, pl.ds(toks, toks)], w_send.at[0], w_recv.at[0], peer(0, True)
    )

    def route_copies(d, other):
        slot, side = (chips - d) % chips, int(other)
        where = peer(d, other)
        return (
            remote(ids_hbm, ids.at[slot, side], i_send.at[d, side], i_recv.at[slot, side], where),
            remote(
                probs_hbm, probs.at[slot, side], p_send.at[d, side], p_recv.at[slot, side], where
            ),
        )

    def forward_copy(j, q):
        return remote(
            tok.at[j, pl.ds(0, toks), cols_of(q)], tok.at[j, pl.ds(toks, toks), cols_of(q)],
            f_send.at[j, q], t_recv.at[j, 1, q], peer(0, True),
        )

    def tok_arrival(j, side, q):
        span = tok.at[j, pl.ds(side * toks, toks), cols_of(q)]
        return remote(span, span, f_send.at[j, q], t_recv.at[j, side, q], peer(0, True))

    def route_arrivals(j, side):
        where = peer(0, True)
        return (
            remote(ids_hbm, ids.at[j, side], i_send.at[0, 1], i_recv.at[j, side], where),
            remote(probs_hbm, probs.at[j, side], p_send.at[0, 1], p_recv.at[j, side], where),
        )

    others = [(d, other) for d in range(chips) for other in (False, True) if d or other]

    for d, other in others:
        for copy in route_copies(d, other):
            copy.start()
    for q in range(parts):
        for d in range(1, chips):
            tok_copy(d, q).start()
        if q == 0:
            twin_copy.start()

    @pl.when(now > 0)
    def _():
        pl.semaphore_signal(z_ready, inc=1, device_id={"tm": now - 1}, device_id_type=MESH)

    for e in range(local):
        for kind in range(2):
            up_copy(kind, e).start()
    for e in range(local):
        down_copy(e).start()
    load_start.start()

    load_ids.wait()
    load_probs.wait()

    local8 = -(-local // 8) * 8
    earlier = jnp.where(
        lax.broadcasted_iota(jnp.int32, (toks, toks), 0)
        < lax.broadcasted_iota(jnp.int32, (toks, toks), 1),
        1.0, 0.0,
    ).astype(BF16)
    rid = lax.broadcasted_iota(jnp.int32, (slots, toks), 0).astype(F32)
    names = me * local + lax.broadcasted_iota(jnp.int32, (local8, toks), 0)
    step_now = step_in[0]

    def place(id_ref, prob_ref):
        member = jnp.zeros((local8, toks), F32)
        weight = jnp.zeros((local8, toks), F32)
        total = jnp.zeros((1, toks), F32)
        for k in range(topk):
            hit = id_ref[k] == names
            member = member + jnp.where(hit, 1.0, 0.0)
            weight = weight + jnp.where(hit, prob_ref[k], 0.0)
            total = total + prob_ref[k]
        count = jnp.dot(member.astype(BF16), earlier, preferred_element_type=F32)
        return jnp.where(member > 0.0, count, -4096.0), weight * (step_now / total)

    def tables(j, carry):
        near = place(ids.at[j, 0], probs.at[j, 0])
        far = place(ids.at[j, 1], probs.at[j, 1])
        for e in range(local):
            low = rid == near[0][e : e + 1, :]
            high = (rid - cap) == far[0][e : e + 1, :]
            mmap[j, e * slots : (e + 1) * slots, :] = jnp.concatenate(
                [jnp.where(low, 1.0, 0.0), jnp.where(high, 1.0, 0.0)], axis=1
            ).astype(BF16)
            share = jnp.sum(
                jnp.where(low, near[1][e : e + 1, :], 0.0)
                + jnp.where(high, far[1][e : e + 1, :], 0.0),
                axis=1, keepdims=True,
            )
            amount[j, e] = jnp.broadcast_to(share, (slots, 128))
        return carry

    for copy in route_arrivals(0, 1):
        copy.wait_recv()
    tables(0, 0)

    def far_tables(j, carry):
        for side in range(2):
            for copy in route_arrivals(j, side):
                copy.wait_recv()
        return tables(j, carry)

    lax.fori_loop(1, chips, far_tables, 0)

    def pass_on(q):
        for j in range(1, chips):
            tok_arrival(j, 0, q).wait_recv()
            forward_copy(j, q).start()

    def loop(first, last, body):
        if last - first == 1:
            body(first, 0)
        else:
            lax.fori_loop(first, last, body, 0)

    def silu_mul(gate, up, j, e):
        return (gate / (1.0 + jnp.exp(-gate)) * (up * amount[j, e, :, 0:1])).astype(BF16)

    def own_rows(e):
        for kind in range(2):
            up_copy(kind, e).wait()
        rows_own[...] = jnp.dot(
            mmap[0, e * slots : (e + 1) * slots, :], tok[0], preferred_element_type=F32
        ).astype(BF16)
        gate = jnp.dot(rows_own[...], wg[e], preferred_element_type=F32)
        up = jnp.dot(rows_own[...], wu[e], preferred_element_type=F32)
        hid[0, e] = silu_mul(gate, up, 0, e)

    def pick(q):
        for j in range(1, chips):
            tok_arrival(j, 1, q).wait_recv()
        lo, hi = cuts[q], cuts[q + 1]

        def one(j, carry):
            rows_far[j - 1, :, lo:hi] = jnp.dot(
                mmap[j], tok[j, :, lo:hi], preferred_element_type=F32
            ).astype(BF16)
            return carry

        loop(1, chips, one)

    def far_rows(q, e):
        lo, hi = cuts[q], cuts[q + 1]

        def one(j, carry):
            piece = rows_far[j - 1, e * slots : (e + 1) * slots, lo:hi]
            gate = jnp.dot(piece, wg[e, lo:hi, :], preferred_element_type=F32)
            up = jnp.dot(piece, wu[e, lo:hi, :], preferred_element_type=F32)
            if q:
                gate = gate + acc_g[j - 1, e]
                up = up + acc_u[j - 1, e]
            if q < parts - 1:
                acc_g[j - 1, e] = gate
                acc_u[j - 1, e] = up
            else:
                hid[j, e] = silu_mul(gate, up, j, e)
            return carry

        loop(1, chips, one)

    twin_copy.wait_recv()

    ready_w = [5.0 + 1.9 * e for e in range(local)]
    near = [2.9 + 11.2 * cuts[q + 1] / width + 2.2 for q in range(parts)]
    todo_own = list(range(local))
    todo_far = [(q, e) for q in range(parts) for e in range(local)]
    clock, passed, picked = 4.9, 0, 0
    while todo_own or todo_far:
        while passed < parts and clock >= near[passed] - 0.2:
            pass_on(passed)
            passed += 1
        own_at = ready_w[todo_own[0]] if todo_own else 1e9
        fit_far = [
            t for t in todo_far
            if max(near[t[0]] + 1.0, ready_w[t[1]]) <= clock and t[1] not in todo_own
        ]
        if todo_own and (own_at <= clock or not fit_far):
            e = todo_own.pop(0)
            own_rows(e)
            clock = max(clock, own_at) + 1.4
            continue
        q, e = fit_far[0] if fit_far else todo_far[0]
        todo_far.remove((q, e))
        while passed <= q:
            pass_on(passed)
            passed += 1
        if picked <= q:
            pick(q)
            picked += 1
        clock = max(clock, near[q] + 1.0, ready_w[e]) + 1.3 * (cuts[q + 1] - cuts[q]) / width
        far_rows(q, e)

    for e in range(local):
        down_copy(e).wait()
    load_start.wait()

    def pair_copy(j, k):
        return remote(
            px_out.at[j, k], px_in.at[j, k], px_send.at[j, k], px_recv.at[j, k], peer(0, True)
        )

    def back_copy(j, k):
        slot = chips - j
        return remote(
            y_out.at[j, k], y_in.at[slot, k], y_send.at[j, k], y_recv.at[slot, k], peer(j, False)
        )

    def rise_copy(k):
        return remote(
            z_out.at[k], z_in.at[k], z_send.at[k], z_recv.at[k], {"tm": lax.rem(now + 1, steps)}
        )

    def down(k, first, last):
        cols = pl.ds(pl.multiple_of(k * dc, 128), dc)

        def one(j, carry):
            for e in range(local):
                ycat[e * slots : (e + 1) * slots, :] = jnp.dot(
                    hid[j, e], wd[e, :, cols], preferred_element_type=F32
                ).astype(BF16)
            share = lax.dot_general(
                mmap[j], ycat[...], (((0,), (0,)), ((), ())), preferred_element_type=F32
            )
            px_out[j, k] = share[toks:].astype(BF16)
            keep[j, k] = share[:toks]
            pair_copy(j, k).start()
            return carry

        loop(first, last, one)

    def send_back(k):
        for j in range(1, chips):
            pair_copy(j, k).wait_recv()
            y_out[j, k] = (keep[j, k] + px_in[j, k].astype(F32)).astype(BF16)
            back_copy(j, k).start()

    def finish(k):
        cols = pl.ds(pl.multiple_of(k * dc, 128), dc)
        pair_copy(0, k).wait_recv()
        total = keep[0, k] + px_in[0, k].astype(F32)
        for j in range(1, chips):
            back_copy(chips - j, k).wait_recv()
            total = total + y_in[j, k].astype(F32)
        keep[0, k] = total

        @pl.when(now > 0)
        def _():
            rise_copy(k).wait_recv()
            keep[0, k] = keep[0, k] + z_in[k].astype(F32)

        @pl.when(now < steps - 1)
        def _():
            z_out[k] = keep[0, k].astype(BF16)
            rise_copy(k).start()

        out_ref[:, cols] = keep[0, k] + start[:, cols]

    @pl.when(now < steps - 1)
    def _():
        pl.semaphore_wait(z_ready, 1)

    lag = jnp.minimum(LAG * (now + 1), chunks)

    def step(k, carry):
        down(k, 1, chips)
        down(k, 0, 1)
        send_back(k)

        @pl.when(k >= lag)
        def _():
            finish(k - lag)

        return carry

    lax.fori_loop(0, chunks, step, 0)

    def rest(k, carry):
        finish(k)
        return carry

    lax.fori_loop(chunks - lag, chunks, rest, 0)

    twin_copy.wait_send()
    for d, other in others:
        for copy in route_copies(d, other):
            copy.wait_send()
    for d in range(1, chips):
        for q in range(parts):
            tok_copy(d, q).wait_send()
            forward_copy(d, q).wait_send()

    def drain(k, carry):
        for j in range(chips):
            pair_copy(j, k).wait_send()
            if j:
                back_copy(j, k).wait_send()

        @pl.when(now < steps - 1)
        def _():
            rise_copy(k).wait_send()

        return carry

    lax.fori_loop(0, chunks, drain, 0)


def shards(mesh, tokens, route_ids, route_probs, step_size, start_state, w_gate, w_up, w_down):
    toks, width = tokens.shape[1:]
    topk = route_ids.shape[2]
    local, _, ff = w_gate.shape
    group = mesh.shape["expert"]
    steps = mesh.shape["tm"]
    chips = group // 2
    cap = 3 * toks * topk // (2 * local * group)
    slots = -(-2 * cap // 16) * 16
    dc = fit(width, DC)
    chunks = width // dc
    cuts = tuple(width * q // PARTS for q in range(PARTS + 1))

    smem = pl.BlockSpec(memory_space=pltpu.SMEM)
    hbm = pl.BlockSpec(memory_space=pl.ANY)
    dma = pltpu.SemaphoreType.DMA
    total = pl.pallas_call(
        functools.partial(kernel, (chips, steps, cap, slots, cuts, dc)),
        out_shape=pltpu.MemorySpace.VMEM((toks, width), F32),
        in_specs=[hbm, hbm, hbm, smem, hbm, hbm, hbm, hbm],
        out_specs=pl.BlockSpec(memory_space=pltpu.VMEM),
        scratch_shapes=[
            pltpu.VMEM((local, width, ff), BF16),
            pltpu.VMEM((local, width, ff), BF16),
            pltpu.VMEM((local, ff, width), BF16),
            pltpu.VMEM((toks, width), BF16),
            pltpu.VMEM((chips, 2 * toks, width), BF16),
            pltpu.VMEM((chips, 2, topk, 1, toks), jnp.int32),
            pltpu.VMEM((chips, 2, topk, 1, toks), F32),
            pltpu.VMEM((toks, width), F32),
            pltpu.VMEM((chips, local, slots, 128), F32),
            pltpu.VMEM((slots, width), BF16),
            pltpu.VMEM((chips - 1, local * slots, width), BF16),
            pltpu.VMEM((chips - 1, local, slots, ff), F32),
            pltpu.VMEM((chips - 1, local, slots, ff), F32),
            pltpu.VMEM((chips, local, slots, ff), BF16),
            pltpu.VMEM((chips, local * slots, 2 * toks), BF16),
            pltpu.VMEM((local * slots, dc), BF16),
            pltpu.VMEM((chips, chunks, toks, dc), F32),
            pltpu.VMEM((chips, chunks, toks, dc), BF16),
            pltpu.VMEM((chips, chunks, toks, dc), BF16),
            pltpu.VMEM((chips, chunks, toks, dc), BF16),
            pltpu.VMEM((chips, chunks, toks, dc), BF16),
            pltpu.VMEM((chunks, toks, dc), BF16),
            pltpu.VMEM((chunks, toks, dc), BF16),
            dma((4,)),
            dma((2, local)),
            dma((local,)),
            dma((chips, PARTS)),
            dma((chips, PARTS)),
            dma((chips, 2, PARTS)),
            dma((1,)),
            dma((1,)),
            dma((chips, 2)),
            dma((chips, 2)),
            dma((chips, 2)),
            dma((chips, 2)),
            dma((chips, chunks)),
            dma((chips, chunks)),
            dma((chips, chunks)),
            dma((chips, chunks)),
            dma((chunks,)),
            dma((chunks,)),
            pltpu.SemaphoreType.REGULAR,
        ],
        compiler_params=pltpu.CompilerParams(
            collective_id=0, has_side_effects=True, vmem_limit_bytes=65_900_000
        ),
    )(
        tokens[0], jnp.transpose(route_ids, (2, 0, 1)), jnp.transpose(route_probs, (2, 0, 1)),
        step_size, start_state, w_gate, w_up, w_down,
    )
    return total[None]


def solution(mesh):
    return jax.shard_map(
        functools.partial(shards, mesh),
        mesh=mesh,
        in_specs=(
            P("tm", ("copies", "expert"), None),
            P("tm", ("copies", "expert"), None),
            P("tm", ("copies", "expert"), None),
            P(("copies", "tm")),
            P(("copies", "expert"), None),
            P("expert", None, None),
            P("expert", None, None),
            P("expert", None, None),
        ),
        out_specs=P("tm", ("copies", "expert"), None),
        check_vma=False,
    )
```

```python
import functools

import jax
import jax.numpy as jnp
from jax import lax
from jax.experimental import pallas as pl
from jax.experimental.pallas import tpu as pltpu
from jax.sharding import PartitionSpec as P

MESH = pl.DeviceIdType.MESH
BF16 = jnp.bfloat16
F32 = jnp.float32
CUTS = (0, 4, 8, 12, 16)
PARTS = len(CUTS) - 1
DC = 256
SPLIT = (2, 2, 4)
PIECES = max(SPLIT)
UNROLL = 4


def fit(total, wanted):
    return wanted if total % wanted == 0 else total


def kernel(
    dims,
    tok_hbm, ids_hbm, probs_hbm, step_in, start_hbm, wg_hbm, wu_hbm, wd_hbm, out_ref,
    wg, wu, wd, raw, tok, ids, probs, start, amount, rows, acc_g, acc_u, hid,
    mmap, ycat,
    keep, px_out, px_in, y_out, y_in, z_out, z_in,
    in_sem, up_sem, down_sem, t_send, f_send, t_recv, w_send, w_recv, i_send, i_recv,
    p_send, p_recv, px_send, px_recv, y_send, y_recv, z_send, z_recv, z_ready,
):
    chips, steps, cap, slots, cuts, dc = dims
    local, width, ff = wg.shape
    toks = start.shape[0]
    topk = ids.shape[2]
    parts = len(cuts) - 1
    chunks = width // dc
    me = lax.axis_index("expert")
    now = lax.axis_index("tm")
    core = lax.rem(me, 2)
    chip = lax.div(me, 2)

    def peer(offset, other):
        own = (1 - core) if other else core
        return {"expert": lax.rem(chip + offset, chips) * 2 + own}

    def remote(src, dst, send, recv, where):
        return pltpu.make_async_remote_copy(
            src_ref=src, dst_ref=dst, send_sem=send, recv_sem=recv,
            device_id=where, device_id_type=MESH,
        )

    def up_copy(kind, e):
        src, dst = ((wg_hbm, wg), (wu_hbm, wu))[kind]
        return pltpu.make_async_copy(src.at[e], dst.at[e], up_sem.at[kind, e])

    def down_copy(e):
        return pltpu.make_async_copy(wd_hbm.at[e], wd.at[e], down_sem.at[e])

    load_tok = pltpu.make_async_copy(tok_hbm, raw, in_sem.at[0])
    load_ids = pltpu.make_async_copy(ids_hbm, ids.at[0, 0], in_sem.at[1])
    load_probs = pltpu.make_async_copy(probs_hbm, probs.at[0, 0], in_sem.at[2])
    load_start = pltpu.make_async_copy(start_hbm, start, in_sem.at[3])

    load_tok.start()
    load_ids.start()
    load_probs.start()
    for kind in range(2):
        up_copy(kind, 0).start()

    barrier = pltpu.get_barrier_semaphore()
    for d in range(chips):
        for other in (False, True):
            if d or other:
                pl.semaphore_signal(barrier, inc=1, device_id=peer(d, other), device_id_type=MESH)

    @pl.when(now < steps - 1)
    def _():
        pl.semaphore_signal(barrier, inc=1, device_id={"tm": now + 1}, device_id_type=MESH)

    load_tok.wait()

    def norm(i, carry):
        span = pl.ds(pl.multiple_of(i * 16, 16), 16)
        values = raw[span, :].astype(F32)
        root = lax.rsqrt(jnp.sum(values * values, axis=1, keepdims=True) * (1.0 / width) + 1e-06)
        tok[0, span, :] = (values * root).astype(BF16)
        return carry

    lax.fori_loop(0, toks // 16, norm, 0, unroll=2)
    pl.semaphore_wait(barrier, 2 * chips - 1 + jnp.where(now > 0, 1, 0))

    def cols_of(q):
        return pl.ds(cuts[q], cuts[q + 1] - cuts[q])

    def tok_copy(d, q):
        slot = (chips - d) % chips
        return remote(
            tok.at[0, pl.ds(0, toks), cols_of(q)], tok.at[slot, pl.ds(0, toks), cols_of(q)],
            t_send.at[d, q], t_recv.at[slot, 0, q], peer(d, False),
        )

    twin_copy = remote(
        tok.at[0, pl.ds(0, toks)], tok.at[0, pl.ds(toks, toks)], w_send.at[0], w_recv.at[0], peer(0, True)
    )

    def route_copies(d, other):
        slot, side = (chips - d) % chips, int(other)
        where = peer(d, other)
        return (
            remote(ids_hbm, ids.at[slot, side], i_send.at[d, side], i_recv.at[slot, side], where),
            remote(
                probs_hbm, probs.at[slot, side], p_send.at[d, side], p_recv.at[slot, side], where
            ),
        )

    def forward_copy(j, q):
        return remote(
            tok.at[j, pl.ds(0, toks), cols_of(q)], tok.at[j, pl.ds(toks, toks), cols_of(q)],
            f_send.at[j, q], t_recv.at[j, 1, q], peer(0, True),
        )

    def tok_arrival(j, side, q):
        span = tok.at[j, pl.ds(side * toks, toks), cols_of(q)]
        return remote(span, span, f_send.at[j, q], t_recv.at[j, side, q], peer(0, True))

    def route_arrivals(j, side):
        where = peer(0, True)
        return (
            remote(ids_hbm, ids.at[j, side], i_send.at[0, 1], i_recv.at[j, side], where),
            remote(probs_hbm, probs.at[j, side], p_send.at[0, 1], p_recv.at[j, side], where),
        )

    others = [(d, other) for d in range(chips) for other in (False, True) if d or other]

    for d, other in others:
        for copy in route_copies(d, other):
            copy.start()
    for q in range(parts):
        for d in range(1, chips):
            tok_copy(d, q).start()
        if q == 0:
            twin_copy.start()

    @pl.when(now > 0)
    def _():
        pl.semaphore_signal(z_ready, inc=1, device_id={"tm": now - 1}, device_id_type=MESH)

    for e in range(1, local):
        for kind in range(2):
            up_copy(kind, e).start()
    for e in range(local):
        down_copy(e).start()
    load_start.start()

    load_ids.wait()
    load_probs.wait()

    local8 = -(-local // 8) * 8
    earlier = jnp.where(
        lax.broadcasted_iota(jnp.int32, (toks, toks), 0)
        < lax.broadcasted_iota(jnp.int32, (toks, toks), 1),
        1.0, 0.0,
    ).astype(BF16)
    rid = lax.broadcasted_iota(jnp.int32, (slots, toks), 0).astype(F32)
    names = me * local + lax.broadcasted_iota(jnp.int32, (local8, toks), 0)
    step_now = step_in[0]

    def place(id_ref, prob_ref):
        member = jnp.zeros((local8, toks), F32)
        weight = jnp.zeros((local8, toks), F32)
        total = jnp.zeros((1, toks), F32)
        for k in range(topk):
            hit = id_ref[k] == names
            member = member + jnp.where(hit, 1.0, 0.0)
            weight = weight + jnp.where(hit, prob_ref[k], 0.0)
            total = total + prob_ref[k]
        count = jnp.dot(member.astype(BF16), earlier, preferred_element_type=F32)
        return jnp.where(member > 0.0, count, -4096.0), weight * (step_now / total)

    def tables(j, carry):
        near = place(ids.at[j, 0], probs.at[j, 0])
        far = place(ids.at[j, 1], probs.at[j, 1])
        for e in range(local):
            low = rid == near[0][e : e + 1, :]
            high = (rid - cap) == far[0][e : e + 1, :]
            mmap[j, e * slots : (e + 1) * slots, :] = jnp.concatenate(
                [jnp.where(low, 1.0, 0.0), jnp.where(high, 1.0, 0.0)], axis=1
            ).astype(BF16)
            share = jnp.sum(
                jnp.where(low, near[1][e : e + 1, :], 0.0)
                + jnp.where(high, far[1][e : e + 1, :], 0.0),
                axis=1, keepdims=True,
            )
            amount[j, e] = jnp.broadcast_to(share, (slots, 128))
        return carry

    for copy in route_arrivals(0, 1):
        copy.wait_recv()
    tables(0, 0)

    def far_tables(j, carry):
        for side in range(2):
            for copy in route_arrivals(j, side):
                copy.wait_recv()
        return tables(j, carry)

    def pass_on(q):
        for j in range(1, chips):
            tok_arrival(j, 0, q).wait_recv()
            forward_copy(j, q).start()

    def loop(first, last, body):
        if last - first == 1:
            body(first, 0)
        else:
            lax.fori_loop(first, last, body, 0)

    def silu_mul(gate, up, j, e):
        return (gate / (1.0 + jnp.exp(-gate)) * (up * amount[j, e, :, 0:1])).astype(BF16)

    def own_rows(e, carry):
        @pl.when(e == local // 2)
        def _():
            loop(1, chips, far_tables)
            pass_on(0)

        for kind in range(2):
            up_copy(kind, e).wait()
        piece = rows[0, pl.ds(pl.multiple_of(e * slots, 16), slots), :]
        gate = jnp.dot(piece, wg[e], preferred_element_type=F32)
        up = jnp.dot(piece, wu[e], preferred_element_type=F32)
        hid[0, e] = silu_mul(gate, up, 0, e)
        return carry

    def pick(first, last, lo, hi):
        def one(j, carry):
            rows[j, :, lo:hi] = jnp.dot(
                mmap[j], tok[j, :, lo:hi], preferred_element_type=F32
            ).astype(BF16)
            return carry

        loop(first, last, one)

    def far_rows(q):
        for j in range(1, chips):
            tok_arrival(j, 1, q).wait_recv()
        lo, hi = cuts[q], cuts[q + 1]
        pick(1, chips, lo, hi)

        def one(j, carry):
            def expert(e, c2):
                piece = rows[j, pl.ds(pl.multiple_of(e * slots, 16), slots), lo:hi]
                gate = jnp.dot(piece, wg[e, lo:hi, :], preferred_element_type=F32)
                up = jnp.dot(piece, wu[e, lo:hi, :], preferred_element_type=F32)
                if q:
                    gate = gate + acc_g[j - 1, e]
                    up = up + acc_u[j - 1, e]
                if q < parts - 1:
                    acc_g[j - 1, e] = gate
                    acc_u[j - 1, e] = up
                else:
                    hid[j, e] = silu_mul(gate, up, j, e)
                return c2

            return lax.fori_loop(0, local, expert, carry, unroll=min(UNROLL, local))

        loop(1, chips, one)

    def pair_copy(j, k):
        return remote(
            px_out.at[j, k], px_in.at[j, k], px_send.at[j, k], px_recv.at[j, k], peer(0, True)
        )

    def bits_of(n):
        return [(p * toks // n, toks // n, p) for p in range(n)]

    tail = SPLIT[-min(len(SPLIT), chunks - 2) :]
    plain = chunks - len(tail)

    def back_copy(j, k, p):
        slot, span, at = chips - j, pl.ds(p[0], p[1]), p[2]
        return remote(
            y_out.at[j, k, span], y_in.at[slot, k, span], y_send.at[j, k, at],
            y_recv.at[slot, k, at], peer(j, False),
        )

    def rise_copy(k, p):
        span, at = pl.ds(p[0], p[1]), p[2]
        return remote(
            z_out.at[k, span], z_in.at[k, span], z_send.at[k, at], z_recv.at[k, at],
            {"tm": lax.rem(now + 1, steps)},
        )

    def down(k, first, last):
        cols = pl.ds(pl.multiple_of(k * dc, 128), dc)

        def one(j, carry):
            for e in range(local):
                ycat[e * slots : (e + 1) * slots, :] = jnp.dot(
                    hid[j, e], wd[e, :, cols], preferred_element_type=F32
                ).astype(BF16)
            share = lax.dot_general(
                mmap[j], ycat[...], (((0,), (0,)), ((), ())), preferred_element_type=F32
            )
            px_out[j, k] = share[toks:].astype(BF16)
            keep[j, k] = share[:toks]
            pair_copy(j, k).start()
            return carry

        loop(first, last, one)

    def send_back(k, n=1):
        for j in range(1, chips):
            pair_copy(j, k).wait_recv()
            for p in bits_of(n):
                span = pl.ds(p[0], p[1])
                y_out[j, k, span, :] = (
                    keep[j, k, span, :] + px_in[j, k, span, :].astype(F32)
                ).astype(BF16)
                back_copy(j, k, p).start()

    def finish(k, n=1):
        cols = pl.ds(pl.multiple_of(k * dc, 128), dc)
        pair_copy(0, k).wait_recv()
        for p in bits_of(n):
            span = pl.ds(p[0], p[1])
            total = keep[0, k, span, :] + px_in[0, k, span, :].astype(F32)
            for j in range(1, chips):
                back_copy(chips - j, k, p).wait_recv()
                total = total + y_in[j, k, span, :].astype(F32)
            keep[0, k, span, :] = total

            @pl.when(now > 0)
            def _():
                rise_copy(k, p).wait_recv()
                keep[0, k, span, :] = keep[0, k, span, :] + z_in[k, span, :].astype(F32)

            @pl.when(now < steps - 1)
            def _():
                z_out[k, span, :] = keep[0, k, span, :].astype(BF16)
                rise_copy(k, p).start()

            out_ref[span, cols] = keep[0, k, span, :] + start[span, cols]

    twin_copy.wait_recv()
    pick(0, 1, 0, width)
    lax.fori_loop(0, local, own_rows, 0)
    passed, early = 1, 0
    for q in range(parts):
        while passed < parts and passed <= q + 1 and passed < parts - 1 or passed <= q:
            pass_on(passed)
            passed += 1
        far_rows(q)
        if q == max(parts - 3, 0):
            for e in range(local):
                down_copy(e).wait()
    load_start.wait()

    down(0, 1, chips)
    down(1, 1, chips)

    def far_step(k, carry):
        down(k, 1, chips)
        send_back(k - 2)
        return carry

    def own_step(k, carry):
        down(k + early, 0, 1)
        finish(k)
        return carry

    lax.fori_loop(2, plain + 2, far_step, 0)
    for i, n in enumerate(tail):
        k = plain + i
        if k + 2 < chunks:
            down(k + 2, 1, chips)
        elif early < 2:
            down(early, 0, 1)
            early += 1
        send_back(k, n)

    @pl.when(now < steps - 1)
    def _():
        pl.semaphore_wait(z_ready, 1)

    lax.fori_loop(0, plain, own_step, 0)
    for i, n in enumerate(tail):
        k = plain + i
        if k + early < chunks:
            down(k + early, 0, 1)
        finish(k, n)

    twin_copy.wait_send()
    for d, other in others:
        for copy in route_copies(d, other):
            copy.wait_send()
    for d in range(1, chips):
        for q in range(parts):
            tok_copy(d, q).wait_send()
            forward_copy(d, q).wait_send()

    def drain(k, carry):
        for j in range(chips):
            pair_copy(j, k).wait_send()

        return carry

    lax.fori_loop(0, chunks, drain, 0)

    def drain_far(k, n):
        for p in bits_of(n):
            for j in range(1, chips):
                back_copy(j, k, p).wait_send()

            @pl.when(now < steps - 1)
            def _():
                rise_copy(k, p).wait_send()

    def drain_one(k, carry):
        drain_far(k, 1)
        return carry

    lax.fori_loop(0, plain, drain_one, 0)
    for i, n in enumerate(tail):
        drain_far(plain + i, n)


def shards(mesh, tokens, route_ids, route_probs, step_size, start_state, w_gate, w_up, w_down):
    toks, width = tokens.shape[1:]
    topk = route_ids.shape[2]
    local, _, ff = w_gate.shape
    group = mesh.shape["expert"]
    steps = mesh.shape["tm"]
    chips = group // 2
    cap = 3 * toks * topk // (2 * local * group)
    slots = -(-2 * cap // 16) * 16
    dc = fit(width, DC)
    chunks = width // dc
    cuts = tuple(width * q // 16 for q in CUTS)

    smem = pl.BlockSpec(memory_space=pltpu.SMEM)
    hbm = pl.BlockSpec(memory_space=pl.ANY)
    dma = pltpu.SemaphoreType.DMA
    total = pl.pallas_call(
        functools.partial(kernel, (chips, steps, cap, slots, cuts, dc)),
        out_shape=pltpu.MemorySpace.VMEM((toks, width), F32),
        in_specs=[hbm, hbm, hbm, smem, hbm, hbm, hbm, hbm],
        out_specs=pl.BlockSpec(memory_space=pltpu.VMEM),
        scratch_shapes=[
            pltpu.VMEM((local, width, ff), BF16),
            pltpu.VMEM((local, width, ff), BF16),
            pltpu.VMEM((local, ff, width), BF16),
            pltpu.VMEM((toks, width), BF16),
            pltpu.VMEM((chips, 2 * toks, width), BF16),
            pltpu.VMEM((chips, 2, topk, 1, toks), jnp.int32),
            pltpu.VMEM((chips, 2, topk, 1, toks), F32),
            pltpu.VMEM((toks, width), F32),
            pltpu.VMEM((chips, local, slots, 128), F32),
            pltpu.VMEM((chips, local * slots, width), BF16),
            pltpu.VMEM((chips - 1, local, slots, ff), F32),
            pltpu.VMEM((chips - 1, local, slots, ff), F32),
            pltpu.VMEM((chips, local, slots, ff), BF16),
            pltpu.VMEM((chips, local * slots, 2 * toks), BF16),
            pltpu.VMEM((local * slots, dc), BF16),
            pltpu.VMEM((chips, chunks, toks, dc), F32),
            pltpu.VMEM((chips, chunks, toks, dc), BF16),
            pltpu.VMEM((chips, chunks, toks, dc), BF16),
            pltpu.VMEM((chips, chunks, toks, dc), BF16),
            pltpu.VMEM((chips, chunks, toks, dc), BF16),
            pltpu.VMEM((chunks, toks, dc), BF16),
            pltpu.VMEM((chunks, toks, dc), BF16),
            dma((4,)),
            dma((2, local)),
            dma((local,)),
            dma((chips, PARTS)),
            dma((chips, PARTS)),
            dma((chips, 2, PARTS)),
            dma((1,)),
            dma((1,)),
            dma((chips, 2)),
            dma((chips, 2)),
            dma((chips, 2)),
            dma((chips, 2)),
            dma((chips, chunks)),
            dma((chips, chunks)),
            dma((chips, chunks, PIECES)),
            dma((chips, chunks, PIECES)),
            dma((chunks, PIECES)),
            dma((chunks, PIECES)),
            pltpu.SemaphoreType.REGULAR,
        ],
        compiler_params=pltpu.CompilerParams(
            collective_id=0, has_side_effects=True, vmem_limit_bytes=65_900_000
        ),
    )(
        tokens[0], jnp.transpose(route_ids, (2, 0, 1)), jnp.transpose(route_probs, (2, 0, 1)),
        step_size, start_state, w_gate, w_up, w_down,
    )
    return total[None]


def solution(mesh):
    return jax.shard_map(
        functools.partial(shards, mesh),
        mesh=mesh,
        in_specs=(
            P("tm", ("copies", "expert"), None),
            P("tm", ("copies", "expert"), None),
            P("tm", ("copies", "expert"), None),
            P(("copies", "tm")),
            P(("copies", "expert"), None),
            P("expert", None, None),
            P("expert", None, None),
            P("expert", None, None),
        ),
        out_specs=P("tm", ("copies", "expert"), None),
        check_vma=False,
    )
```

```python
import functools

import jax
import jax.numpy as jnp
from jax import lax
from jax.experimental import pallas as pl
from jax.experimental.pallas import tpu as pltpu
from jax.sharding import PartitionSpec as P

MESH = pl.DeviceIdType.MESH
BF16 = jnp.bfloat16
F32 = jnp.float32
CUTS = (0, 4, 8, 12, 16)
PARTS = len(CUTS) - 1
DC = 256
SPLIT = (1, 2, 4)
SPARE = sum(SPLIT) - len(SPLIT)
UNROLL = 4


def fit(total, wanted):
    return wanted if total % wanted == 0 else total


def kernel(
    dims,
    tok_hbm, ids_hbm, probs_hbm, step_in, start_hbm, wg_hbm, wu_hbm, wd_hbm, out_ref,
    wg, wu, wd, raw, tok, ids, probs, start, amount, rows, acc_g, acc_u, hid,
    mmap, ycat,
    keep, px_out, px_in, y_out, y_in, z_out, z_in,
    in_sem, up_sem, down_sem, t_send, f_send, t_recv, w_send, w_recv, i_send, i_recv,
    p_send, p_recv, px_send, px_recv, y_send, y_recv, z_send, z_recv, z_ready,
):
    chips, steps, cap, slots, cuts, dc = dims
    local, width, ff = wg.shape
    toks = start.shape[0]
    topk = ids.shape[2]
    parts = len(cuts) - 1
    chunks = width // dc
    me = lax.axis_index("expert")
    now = lax.axis_index("tm")
    core = lax.rem(me, 2)
    chip = lax.div(me, 2)

    def peer(offset, other):
        own = (1 - core) if other else core
        return {"expert": lax.rem(chip + offset, chips) * 2 + own}

    def remote(src, dst, send, recv, where):
        return pltpu.make_async_remote_copy(
            src_ref=src, dst_ref=dst, send_sem=send, recv_sem=recv,
            device_id=where, device_id_type=MESH,
        )

    def up_copy(kind, e):
        src, dst = ((wg_hbm, wg), (wu_hbm, wu))[kind]
        return pltpu.make_async_copy(src.at[e], dst.at[e], up_sem.at[kind, e])

    def down_copy(e):
        return pltpu.make_async_copy(wd_hbm.at[e], wd.at[e], down_sem.at[e])

    load_tok = pltpu.make_async_copy(tok_hbm, raw, in_sem.at[0])
    load_ids = pltpu.make_async_copy(ids_hbm, ids.at[0, 0], in_sem.at[1])
    load_probs = pltpu.make_async_copy(probs_hbm, probs.at[0, 0], in_sem.at[2])
    load_start = pltpu.make_async_copy(start_hbm, start, in_sem.at[3])

    load_tok.start()
    load_ids.start()
    load_probs.start()
    for kind in range(2):
        up_copy(kind, 0).start()

    barrier = pltpu.get_barrier_semaphore()
    for d in range(chips):
        for other in (False, True):
            if d or other:
                pl.semaphore_signal(barrier, inc=1, device_id=peer(d, other), device_id_type=MESH)

    @pl.when(now < steps - 1)
    def _():
        pl.semaphore_signal(barrier, inc=1, device_id={"tm": now + 1}, device_id_type=MESH)

    load_tok.wait()

    def norm(i, carry):
        span = pl.ds(pl.multiple_of(i * 16, 16), 16)
        values = raw[span, :].astype(F32)
        root = lax.rsqrt(jnp.sum(values * values, axis=1, keepdims=True) * (1.0 / width) + 1e-06)
        tok[0, span, :] = (values * root).astype(BF16)
        return carry

    lax.fori_loop(0, toks // 16, norm, 0, unroll=2)
    pl.semaphore_wait(barrier, 2 * chips - 1 + jnp.where(now > 0, 1, 0))

    def cols_of(q):
        return pl.ds(cuts[q], cuts[q + 1] - cuts[q])

    def tok_copy(d, q):
        slot = (chips - d) % chips
        return remote(
            tok.at[0, pl.ds(0, toks), cols_of(q)], tok.at[slot, pl.ds(0, toks), cols_of(q)],
            t_send.at[d, q], t_recv.at[slot, 0, q], peer(d, False),
        )

    twin_copy = remote(
        tok.at[0, pl.ds(0, toks)], tok.at[0, pl.ds(toks, toks)], w_send.at[0], w_recv.at[0], peer(0, True)
    )

    def route_copies(d, other):
        slot, side = (chips - d) % chips, int(other)
        where = peer(d, other)
        return (
            remote(ids_hbm, ids.at[slot, side], i_send.at[d, side], i_recv.at[slot, side], where),
            remote(
                probs_hbm, probs.at[slot, side], p_send.at[d, side], p_recv.at[slot, side], where
            ),
        )

    def forward_copy(j, q):
        return remote(
            tok.at[j, pl.ds(0, toks), cols_of(q)], tok.at[j, pl.ds(toks, toks), cols_of(q)],
            f_send.at[j, q], t_recv.at[j, 1, q], peer(0, True),
        )

    def tok_arrival(j, side, q):
        span = tok.at[j, pl.ds(side * toks, toks), cols_of(q)]
        return remote(span, span, f_send.at[j, q], t_recv.at[j, side, q], peer(0, True))

    def route_arrivals(j, side):
        where = peer(0, True)
        return (
            remote(ids_hbm, ids.at[j, side], i_send.at[0, 1], i_recv.at[j, side], where),
            remote(probs_hbm, probs.at[j, side], p_send.at[0, 1], p_recv.at[j, side], where),
        )

    others = [(d, other) for d in range(chips) for other in (False, True) if d or other]

    for d, other in others:
        for copy in route_copies(d, other):
            copy.start()
    for q in range(parts):
        for d in range(1, chips):
            tok_copy(d, q).start()
        if q == 0:
            twin_copy.start()

    @pl.when(now > 0)
    def _():
        pl.semaphore_signal(z_ready, inc=1, device_id={"tm": now - 1}, device_id_type=MESH)

    for e in range(1, local):
        for kind in range(2):
            up_copy(kind, e).start()
    for e in range(local):
        down_copy(e).start()
    load_start.start()

    load_ids.wait()
    load_probs.wait()

    local8 = -(-local // 8) * 8
    earlier = jnp.where(
        lax.broadcasted_iota(jnp.int32, (toks, toks), 0)
        < lax.broadcasted_iota(jnp.int32, (toks, toks), 1),
        1.0, 0.0,
    ).astype(BF16)
    rid = lax.broadcasted_iota(jnp.int32, (slots, toks), 0).astype(F32)
    names = me * local + lax.broadcasted_iota(jnp.int32, (local8, toks), 0)
    step_now = step_in[0]

    def place(id_ref, prob_ref):
        member = jnp.zeros((local8, toks), F32)
        weight = jnp.zeros((local8, toks), F32)
        total = jnp.zeros((1, toks), F32)
        for k in range(topk):
            hit = id_ref[k] == names
            member = member + jnp.where(hit, 1.0, 0.0)
            weight = weight + jnp.where(hit, prob_ref[k], 0.0)
            total = total + prob_ref[k]
        count = jnp.dot(member.astype(BF16), earlier, preferred_element_type=F32)
        return jnp.where(member > 0.0, count, -4096.0), weight * (step_now / total)

    def tables(j, carry):
        near = place(ids.at[j, 0], probs.at[j, 0])
        far = place(ids.at[j, 1], probs.at[j, 1])
        for e in range(local):
            low = rid == near[0][e : e + 1, :]
            high = (rid - cap) == far[0][e : e + 1, :]
            mmap[j, e * slots : (e + 1) * slots, :] = jnp.concatenate(
                [jnp.where(low, 1.0, 0.0), jnp.where(high, 1.0, 0.0)], axis=1
            ).astype(BF16)
            share = jnp.sum(
                jnp.where(low, near[1][e : e + 1, :], 0.0)
                + jnp.where(high, far[1][e : e + 1, :], 0.0),
                axis=1, keepdims=True,
            )
            amount[j, e] = jnp.broadcast_to(share, (slots, 128))
        return carry

    for copy in route_arrivals(0, 1):
        copy.wait_recv()
    tables(0, 0)

    def far_tables(j, carry):
        for side in range(2):
            for copy in route_arrivals(j, side):
                copy.wait_recv()
        return tables(j, carry)

    def pass_on(q):
        for j in range(1, chips):
            tok_arrival(j, 0, q).wait_recv()
            forward_copy(j, q).start()

    def loop(first, last, body):
        if last - first == 1:
            body(first, 0)
        else:
            lax.fori_loop(first, last, body, 0)

    def silu_mul(gate, up, j, e):
        return (gate / (1.0 + jnp.exp(-gate)) * (up * amount[j, e, :, 0:1])).astype(BF16)

    def own_rows(e, carry):
        @pl.when(e == local // 2)
        def _():
            loop(1, chips, far_tables)
            pass_on(0)

        for kind in range(2):
            up_copy(kind, e).wait()
        piece = rows[0, pl.ds(pl.multiple_of(e * slots, 16), slots), :]
        gate = jnp.dot(piece, wg[e], preferred_element_type=F32)
        up = jnp.dot(piece, wu[e], preferred_element_type=F32)
        hid[0, e] = silu_mul(gate, up, 0, e)
        return carry

    def pick(first, last, lo, hi):
        def one(j, carry):
            rows[j, :, lo:hi] = jnp.dot(
                mmap[j], tok[j, :, lo:hi], preferred_element_type=F32
            ).astype(BF16)
            return carry

        loop(first, last, one)

    def far_rows(q):
        for j in range(1, chips):
            tok_arrival(j, 1, q).wait_recv()
        lo, hi = cuts[q], cuts[q + 1]
        pick(1, chips, lo, hi)

        def one(j, carry):
            def expert(e, c2):
                piece = rows[j, pl.ds(pl.multiple_of(e * slots, 16), slots), lo:hi]
                gate = jnp.dot(piece, wg[e, lo:hi, :], preferred_element_type=F32)
                up = jnp.dot(piece, wu[e, lo:hi, :], preferred_element_type=F32)
                if q:
                    gate = gate + acc_g[j - 1, e]
                    up = up + acc_u[j - 1, e]
                if q < parts - 1:
                    acc_g[j - 1, e] = gate
                    acc_u[j - 1, e] = up
                else:
                    hid[j, e] = silu_mul(gate, up, j, e)
                return c2

            return lax.fori_loop(0, local, expert, carry, unroll=min(UNROLL, local))

        loop(1, chips, one)

    def pair_copy(j, k):
        return remote(
            px_out.at[j, k], px_in.at[j, k], px_send.at[j, k], px_recv.at[j, k], peer(0, True)
        )

    whole = ((0, toks, None),)
    tail = []
    spare = chunks
    for n in SPLIT:
        tail.append([(p * toks // n, toks // n, spare + p - 1 if p else None) for p in range(n)])
        spare += n - 1
    plain = chunks - len(tail)

    def back_copy(j, k, p):
        slot, span, at = chips - j, pl.ds(p[0], p[1]), k if p[2] is None else p[2]
        return remote(
            y_out.at[j, k, span], y_in.at[slot, k, span], y_send.at[j - 1, at],
            y_recv.at[slot - 1, at], peer(j, False),
        )

    def rise_copy(k, p):
        span, at = pl.ds(p[0], p[1]), k if p[2] is None else p[2]
        return remote(
            z_out.at[k, span], z_in.at[k, span], z_send.at[at], z_recv.at[at],
            {"tm": lax.rem(now + 1, steps)},
        )

    def down(k, first, last):
        cols = pl.ds(pl.multiple_of(k * dc, 128), dc)

        def one(j, carry):
            for e in range(local):
                ycat[e * slots : (e + 1) * slots, :] = jnp.dot(
                    hid[j, e], wd[e, :, cols], preferred_element_type=F32
                ).astype(BF16)
            share = lax.dot_general(
                mmap[j], ycat[...], (((0,), (0,)), ((), ())), preferred_element_type=F32
            )
            px_out[j, k] = share[toks:].astype(BF16)
            keep[j, k] = share[:toks]
            pair_copy(j, k).start()
            return carry

        loop(first, last, one)

    def send_back(k, bits=whole):
        for j in range(1, chips):
            pair_copy(j, k).wait_recv()
            for p in bits:
                span = pl.ds(p[0], p[1])
                y_out[j, k, span, :] = (
                    keep[j, k, span, :] + px_in[j, k, span, :].astype(F32)
                ).astype(BF16)
                back_copy(j, k, p).start()

    def finish(k, bits=whole):
        cols = pl.ds(pl.multiple_of(k * dc, 128), dc)
        pair_copy(0, k).wait_recv()
        for p in bits:
            span = pl.ds(p[0], p[1])
            total = keep[0, k, span, :] + px_in[0, k, span, :].astype(F32)
            for j in range(1, chips):
                back_copy(chips - j, k, p).wait_recv()
                total = total + y_in[j, k, span, :].astype(F32)
            keep[0, k, span, :] = total

            @pl.when(now > 0)
            def _():
                rise_copy(k, p).wait_recv()
                keep[0, k, span, :] = keep[0, k, span, :] + z_in[k, span, :].astype(F32)

            @pl.when(now < steps - 1)
            def _():
                z_out[k, span, :] = keep[0, k, span, :].astype(BF16)
                rise_copy(k, p).start()

            out_ref[span, cols] = keep[0, k, span, :] + start[span, cols]

    twin_copy.wait_recv()
    pick(0, 1, 0, width)
    lax.fori_loop(0, local, own_rows, 0)
    passed = 1
    for q in range(parts):
        while passed < parts and passed <= q + 1 and passed < parts - 1 or passed <= q:
            pass_on(passed)
            passed += 1
        far_rows(q)
    for e in range(local):
        down_copy(e).wait()
    load_start.wait()

    @pl.when(now < steps - 1)
    def _():
        pl.semaphore_wait(z_ready, 1)

    first = now == 0
    down(0, 1, chips)
    down(1, 1, chips)

    def far_step(k, carry):
        down(k, 1, chips)
        send_back(k - 2)

        @pl.when((k == 3) | (k == 4))
        def _():
            down(k - 3, 0, 1)

        @pl.when(first & (k == 5))
        def _():
            finish(0)

        return carry

    lax.fori_loop(2, plain + 2, far_step, 0)
    for i, n in enumerate(tail):
        k = plain + i
        if k + 2 < chunks:
            down(k + 2, 1, chips)
        send_back(k, n)
        if i == 0:

            @pl.when(first)
            def _():
                finish(1)

        else:
            down(1 + i, 0, 1)

    def own_step(k, carry):
        @pl.when(k >= len(tail) - 1)
        def _():
            down(k + 2, 0, 1)

        finish(k)
        return carry

    lax.fori_loop(jnp.where(first, 2, 0), plain, own_step, 0)
    for i, n in enumerate(tail):
        k = plain + i
        if k + 2 < chunks:
            down(k + 2, 0, 1)
        finish(k, n)

    twin_copy.wait_send()
    for d, other in others:
        for copy in route_copies(d, other):
            copy.wait_send()
    for d in range(1, chips):
        for q in range(parts):
            tok_copy(d, q).wait_send()
            forward_copy(d, q).wait_send()

    def drain(k, carry):
        for j in range(chips):
            pair_copy(j, k).wait_send()

        return carry

    lax.fori_loop(0, chunks, drain, 0)

    def drain_far(k, bits):
        for p in bits:
            for j in range(1, chips):
                back_copy(j, k, p).wait_send()

            @pl.when(now < steps - 1)
            def _():
                rise_copy(k, p).wait_send()

    def drain_one(k, carry):
        drain_far(k, whole)
        return carry

    lax.fori_loop(0, plain, drain_one, 0)
    for i, n in enumerate(tail):
        drain_far(plain + i, n)


def shards(mesh, tokens, route_ids, route_probs, step_size, start_state, w_gate, w_up, w_down):
    toks, width = tokens.shape[1:]
    topk = route_ids.shape[2]
    local, _, ff = w_gate.shape
    group = mesh.shape["expert"]
    steps = mesh.shape["tm"]
    chips = group // 2
    cap = 3 * toks * topk // (2 * local * group)
    slots = -(-2 * cap // 16) * 16
    dc = fit(width, DC)
    chunks = width // dc
    cuts = tuple(width * q // 16 for q in CUTS)

    smem = pl.BlockSpec(memory_space=pltpu.SMEM)
    hbm = pl.BlockSpec(memory_space=pl.ANY)
    dma = pltpu.SemaphoreType.DMA
    total = pl.pallas_call(
        functools.partial(kernel, (chips, steps, cap, slots, cuts, dc)),
        out_shape=pltpu.MemorySpace.VMEM((toks, width), F32),
        in_specs=[hbm, hbm, hbm, smem, hbm, hbm, hbm, hbm],
        out_specs=pl.BlockSpec(memory_space=pltpu.VMEM),
        scratch_shapes=[
            pltpu.VMEM((local, width, ff), BF16),
            pltpu.VMEM((local, width, ff), BF16),
            pltpu.VMEM((local, ff, width), BF16),
            pltpu.VMEM((toks, width), BF16),
            pltpu.VMEM((chips, 2 * toks, width), BF16),
            pltpu.VMEM((chips, 2, topk, 1, toks), jnp.int32),
            pltpu.VMEM((chips, 2, topk, 1, toks), F32),
            pltpu.VMEM((toks, width), F32),
            pltpu.VMEM((chips, local, slots, 128), F32),
            pltpu.VMEM((chips, local * slots, width), BF16),
            pltpu.VMEM((chips - 1, local, slots, ff), F32),
            pltpu.VMEM((chips - 1, local, slots, ff), F32),
            pltpu.VMEM((chips, local, slots, ff), BF16),
            pltpu.VMEM((chips, local * slots, 2 * toks), BF16),
            pltpu.VMEM((local * slots, dc), BF16),
            pltpu.VMEM((chips, chunks, toks, dc), F32),
            pltpu.VMEM((chips, chunks, toks, dc), BF16),
            pltpu.VMEM((chips, chunks, toks, dc), BF16),
            pltpu.VMEM((chips, chunks, toks, dc), BF16),
            pltpu.VMEM((chips, chunks, toks, dc), BF16),
            pltpu.VMEM((chunks, toks, dc), BF16),
            pltpu.VMEM((chunks, toks, dc), BF16),
            dma((4,)),
            dma((2, local)),
            dma((local,)),
            dma((chips, PARTS)),
            dma((chips, PARTS)),
            dma((chips, 2, PARTS)),
            dma((1,)),
            dma((1,)),
            dma((chips, 2)),
            dma((chips, 2)),
            dma((chips, 2)),
            dma((chips, 2)),
            dma((chips, chunks)),
            dma((chips, chunks)),
            dma((chips - 1, chunks + SPARE)),
            dma((chips - 1, chunks + SPARE)),
            dma((chunks + SPARE,)),
            dma((chunks + SPARE,)),
            pltpu.SemaphoreType.REGULAR,
        ],
        compiler_params=pltpu.CompilerParams(
            collective_id=0, has_side_effects=True, vmem_limit_bytes=65_900_000
        ),
    )(
        tokens[0], jnp.transpose(route_ids, (2, 0, 1)), jnp.transpose(route_probs, (2, 0, 1)),
        step_size, start_state, w_gate, w_up, w_down,
    )
    return total[None]


def solution(mesh):
    return jax.shard_map(
        functools.partial(shards, mesh),
        mesh=mesh,
        in_specs=(
            P("tm", ("copies", "expert"), None),
            P("tm", ("copies", "expert"), None),
            P("tm", ("copies", "expert"), None),
            P(("copies", "tm")),
            P(("copies", "expert"), None),
            P("expert", None, None),
            P("expert", None, None),
            P("expert", None, None),
        ),
        out_specs=P("tm", ("copies", "expert"), None),
        check_vma=False,
    )
```

```python
import functools

import jax
import jax.numpy as jnp
from jax import lax
from jax.experimental import pallas as pl
from jax.experimental.pallas import tpu as pltpu
from jax.sharding import PartitionSpec as P

MESH = pl.DeviceIdType.MESH
BF16 = jnp.bfloat16
F32 = jnp.float32
CUTS = (0, 4, 8, 12, 16)
PARTS = len(CUTS) - 1
DC = 256
SPLIT = (1, 2, 4)
SPARE = sum(SPLIT) - len(SPLIT)
UNROLL = 4


def fit(total, wanted):
    return wanted if total % wanted == 0 else total


def kernel(
    dims,
    tok_hbm, ids_hbm, probs_hbm, step_in, start_hbm, wg_hbm, wu_hbm, wd_hbm, out_ref,
    wg, wu, wd, raw, tok, ids, probs, start, amount, rows, acc_g, acc_u, hid,
    mmap, ycat,
    keep, px_out, px_in, y_out, y_in, z_out, z_in,
    in_sem, up_sem, down_sem, t_send, f_send, t_recv, w_send, w_recv, i_send, i_recv,
    p_send, p_recv, px_send, px_recv, y_send, y_recv, z_send, z_recv, z_ready,
):
    chips, steps, cap, slots, cuts, dc = dims
    local, width, ff = wg.shape
    toks = start.shape[0]
    topk = ids.shape[2]
    parts = len(cuts) - 1
    chunks = width // dc
    me = lax.axis_index("expert")
    now = lax.axis_index("tm")
    core = lax.rem(me, 2)
    chip = lax.div(me, 2)

    def peer(offset, other):
        own = (1 - core) if other else core
        return {"expert": lax.rem(chip + offset, chips) * 2 + own}

    def remote(src, dst, send, recv, where):
        return pltpu.make_async_remote_copy(
            src_ref=src, dst_ref=dst, send_sem=send, recv_sem=recv,
            device_id=where, device_id_type=MESH,
        )

    def up_copy(kind, e):
        src, dst = ((wg_hbm, wg), (wu_hbm, wu))[kind]
        return pltpu.make_async_copy(src.at[e], dst.at[e], up_sem.at[kind, e])

    def down_copy(e):
        return pltpu.make_async_copy(wd_hbm.at[e], wd.at[e], down_sem.at[e])

    load_tok = pltpu.make_async_copy(tok_hbm, raw, in_sem.at[0])
    load_ids = pltpu.make_async_copy(ids_hbm, ids.at[0, 0], in_sem.at[1])
    load_probs = pltpu.make_async_copy(probs_hbm, probs.at[0, 0], in_sem.at[2])
    load_start = pltpu.make_async_copy(start_hbm, start, in_sem.at[3])

    load_tok.start()
    load_ids.start()
    load_probs.start()
    for kind in range(2):
        up_copy(kind, 0).start()

    barrier = pltpu.get_barrier_semaphore()
    for d in range(chips):
        for other in (False, True):
            if d or other:
                pl.semaphore_signal(barrier, inc=1, device_id=peer(d, other), device_id_type=MESH)

    @pl.when(now < steps - 1)
    def _():
        pl.semaphore_signal(barrier, inc=1, device_id={"tm": now + 1}, device_id_type=MESH)

    load_tok.wait()

    def norm(i, carry):
        span = pl.ds(pl.multiple_of(i * 16, 16), 16)
        values = raw[span, :].astype(F32)
        root = lax.rsqrt(jnp.sum(values * values, axis=1, keepdims=True) * (1.0 / width) + 1e-06)
        tok[0, span, :] = (values * root).astype(BF16)
        return carry

    lax.fori_loop(0, toks // 16, norm, 0, unroll=4)
    pl.semaphore_wait(barrier, 2 * chips - 1 + jnp.where(now > 0, 1, 0))

    def cols_of(q):
        return pl.ds(cuts[q], cuts[q + 1] - cuts[q])

    def tok_copy(d, q):
        slot = (chips - d) % chips
        return remote(
            tok.at[0, pl.ds(0, toks), cols_of(q)], tok.at[slot, pl.ds(0, toks), cols_of(q)],
            t_send.at[d - 1, q], t_recv.at[slot - 1, 0, q], peer(d, False),
        )

    twin_copy = remote(
        tok.at[0, pl.ds(0, toks)], tok.at[0, pl.ds(toks, toks)], w_send.at[0], w_recv.at[0], peer(0, True)
    )

    def route_copies(d, other):
        slot, side = (chips - d) % chips, int(other)
        where = peer(d, other)
        return (
            remote(ids_hbm, ids.at[slot, side], i_send.at[d, side], i_recv.at[slot, side], where),
            remote(
                probs_hbm, probs.at[slot, side], p_send.at[d, side], p_recv.at[slot, side], where
            ),
        )

    def forward_copy(j, q):
        return remote(
            tok.at[j, pl.ds(0, toks), cols_of(q)], tok.at[j, pl.ds(toks, toks), cols_of(q)],
            f_send.at[j - 1, q], t_recv.at[j - 1, 1, q], peer(0, True),
        )

    def tok_arrival(j, side, q):
        span = tok.at[j, pl.ds(side * toks, toks), cols_of(q)]
        return remote(
            span, span, f_send.at[j - 1, q], t_recv.at[j - 1, side, q], peer(0, True)
        )

    def route_arrivals(j, side):
        where = peer(0, True)
        return (
            remote(ids_hbm, ids.at[j, side], i_send.at[0, 1], i_recv.at[j, side], where),
            remote(probs_hbm, probs.at[j, side], p_send.at[0, 1], p_recv.at[j, side], where),
        )

    others = [(d, other) for d in range(chips) for other in (False, True) if d or other]

    for d, other in others:
        for copy in route_copies(d, other):
            copy.start()
    for q in range(parts):
        for d in range(1, chips):
            tok_copy(d, q).start()
        if q == 0:
            twin_copy.start()

    @pl.when(now > 0)
    def _():
        pl.semaphore_signal(z_ready, inc=1, device_id={"tm": now - 1}, device_id_type=MESH)

    for e in range(1, local):
        for kind in range(2):
            up_copy(kind, e).start()
    for e in range(local):
        down_copy(e).start()
    load_start.start()

    load_ids.wait()
    load_probs.wait()

    local8 = -(-local // 8) * 8
    earlier = jnp.where(
        lax.broadcasted_iota(jnp.int32, (toks, toks), 0)
        < lax.broadcasted_iota(jnp.int32, (toks, toks), 1),
        1.0, 0.0,
    ).astype(BF16)
    rid = lax.broadcasted_iota(jnp.int32, (slots, toks), 0).astype(F32)
    names = me * local + lax.broadcasted_iota(jnp.int32, (local8, toks), 0)
    step_now = step_in[0]

    def place(id_ref, prob_ref):
        member = jnp.zeros((local8, toks), F32)
        weight = jnp.zeros((local8, toks), F32)
        total = jnp.zeros((1, toks), F32)
        for k in range(topk):
            hit = id_ref[k] == names
            member = member + jnp.where(hit, 1.0, 0.0)
            weight = weight + jnp.where(hit, prob_ref[k], 0.0)
            total = total + prob_ref[k]
        count = jnp.dot(member.astype(BF16), earlier, preferred_element_type=F32)
        return jnp.where(member > 0.0, count, -4096.0), weight * (step_now / total)

    def tables(j, carry):
        near = place(ids.at[j, 0], probs.at[j, 0])
        far = place(ids.at[j, 1], probs.at[j, 1])
        for e in range(local):
            low = rid == near[0][e : e + 1, :]
            high = (rid - cap) == far[0][e : e + 1, :]
            mmap[j, e * slots : (e + 1) * slots, :] = jnp.concatenate(
                [jnp.where(low, 1.0, 0.0), jnp.where(high, 1.0, 0.0)], axis=1
            ).astype(BF16)
            share = jnp.sum(
                jnp.where(low, near[1][e : e + 1, :], 0.0)
                + jnp.where(high, far[1][e : e + 1, :], 0.0),
                axis=1, keepdims=True,
            )
            amount[j, e] = jnp.broadcast_to(share, (slots, 128))
        return carry

    for copy in route_arrivals(0, 1):
        copy.wait_recv()
    tables(0, 0)

    def far_tables(j, carry):
        for side in range(2):
            for copy in route_arrivals(j, side):
                copy.wait_recv()
        return tables(j, carry)

    def pass_on(q):
        for j in range(1, chips):
            tok_arrival(j, 0, q).wait_recv()
            forward_copy(j, q).start()

    def loop(first, last, body):
        if last - first == 1:
            body(first, 0)
        else:
            lax.fori_loop(first, last, body, 0)

    def silu_mul(gate, up, j, e):
        return (gate / (1.0 + jnp.exp(-gate)) * (up * amount[j, e, :, 0:1])).astype(BF16)

    def own_rows(e, carry):
        if e == local // 2:
            loop(1, chips, far_tables)
            pass_on(0)

        for kind in range(2):
            up_copy(kind, e).wait()
        piece = rows[0, pl.ds(pl.multiple_of(e * slots, 16), slots), :]
        gate = jnp.dot(piece, wg[e], preferred_element_type=F32)
        up = jnp.dot(piece, wu[e], preferred_element_type=F32)
        hid[0, e] = silu_mul(gate, up, 0, e)
        return carry

    def pick(first, last, lo, hi):
        def one(j, carry):
            rows[j, :, lo:hi] = jnp.dot(
                mmap[j], tok[j, :, lo:hi], preferred_element_type=F32
            ).astype(BF16)
            return carry

        loop(first, last, one)

    def far_rows(q):
        for j in range(1, chips):
            tok_arrival(j, 1, q).wait_recv()
        lo, hi = cuts[q], cuts[q + 1]
        pick(1, chips, lo, hi)

        def one(j, carry):
            def expert(e, c2):
                piece = rows[j, pl.ds(pl.multiple_of(e * slots, 16), slots), lo:hi]
                gate = jnp.dot(piece, wg[e, lo:hi, :], preferred_element_type=F32)
                up = jnp.dot(piece, wu[e, lo:hi, :], preferred_element_type=F32)
                if q:
                    gate = gate + acc_g[j - 1, e]
                    up = up + acc_u[j - 1, e]
                if q < parts - 1:
                    acc_g[j - 1, e] = gate
                    acc_u[j - 1, e] = up
                else:
                    hid[j, e] = silu_mul(gate, up, j, e)
                return c2

            return lax.fori_loop(0, local, expert, carry, unroll=min(UNROLL, local))

        loop(1, chips, one)

    def pair_copy(j, k):
        return remote(
            px_out.at[j, k], px_in.at[j, k], px_send.at[j, k], px_recv.at[j, k], peer(0, True)
        )

    whole = ((0, toks, None),)
    tail = []
    spare = chunks
    for n in SPLIT:
        tail.append([(p * toks // n, toks // n, spare + p - 1 if p else None) for p in range(n)])
        spare += n - 1
    plain = chunks - len(tail)

    def back_copy(j, k, p):
        slot, span, at = chips - j, pl.ds(p[0], p[1]), k if p[2] is None else p[2]
        return remote(
            y_out.at[j, k, span], y_in.at[slot, k, span], y_send.at[j - 1, at],
            y_recv.at[slot - 1, at], peer(j, False),
        )

    def rise_copy(k, p):
        span, at = pl.ds(p[0], p[1]), k if p[2] is None else p[2]
        return remote(
            z_out.at[k, span], z_in.at[k, span], z_send.at[at], z_recv.at[at],
            {"tm": lax.rem(now + 1, steps)},
        )

    def down(k, first, last):
        cols = pl.ds(pl.multiple_of(k * dc, 128), dc)

        def one(j, carry):
            for e in range(local):
                ycat[e * slots : (e + 1) * slots, :] = jnp.dot(
                    hid[j, e], wd[e, :, cols], preferred_element_type=F32
                ).astype(BF16)
            share = lax.dot_general(
                mmap[j], ycat[...], (((0,), (0,)), ((), ())), preferred_element_type=F32
            )
            px_out[j, k] = share[toks:].astype(BF16)
            keep[j, k] = share[:toks]
            pair_copy(j, k).start()
            return carry

        loop(first, last, one)

    def send_back(k, bits=whole):
        for j in range(1, chips):
            pair_copy(j, k).wait_recv()
            for p in bits:
                span = pl.ds(p[0], p[1])
                y_out[j, k, span, :] = (
                    keep[j, k, span, :] + px_in[j, k, span, :].astype(F32)
                ).astype(BF16)
                back_copy(j, k, p).start()

    def finish(k, bits=whole):
        cols = pl.ds(pl.multiple_of(k * dc, 128), dc)
        pair_copy(0, k).wait_recv()
        for p in bits:
            span = pl.ds(p[0], p[1])
            total = keep[0, k, span, :] + px_in[0, k, span, :].astype(F32)
            for j in range(1, chips):
                back_copy(chips - j, k, p).wait_recv()
                total = total + y_in[j, k, span, :].astype(F32)
            keep[0, k, span, :] = total

            @pl.when(now > 0)
            def _():
                rise_copy(k, p).wait_recv()
                keep[0, k, span, :] = keep[0, k, span, :] + z_in[k, span, :].astype(F32)

            @pl.when(now < steps - 1)
            def _():
                z_out[k, span, :] = keep[0, k, span, :].astype(BF16)
                rise_copy(k, p).start()

            out_ref[span, cols] = keep[0, k, span, :] + start[span, cols]

    twin_copy.wait_recv()
    pick(0, 1, 0, width)
    for e in range(local):
        own_rows(e, 0)
    passed = 1
    for q in range(parts):
        while passed < parts and passed <= q + 1 and passed < parts - 1 or passed <= q:
            pass_on(passed)
            passed += 1
        far_rows(q)
    for e in range(local):
        down_copy(e).wait()
    load_start.wait()

    @pl.when(now < steps - 1)
    def _():
        pl.semaphore_wait(z_ready, 1)

    first = now == 0
    down(0, 1, chips)
    down(1, 1, chips)

    def far_step(k, carry):
        down(k, 1, chips)
        send_back(k - 2)

        @pl.when((k == 3) | (k == 4))
        def _():
            down(k - 3, 0, 1)

        @pl.when(first & (k == 5))
        def _():
            finish(0)

        return carry

    lax.fori_loop(2, plain + 2, far_step, 0)
    for i, n in enumerate(tail):
        k = plain + i
        if k + 2 < chunks:
            down(k + 2, 1, chips)
        send_back(k, n)
        if i == 0:

            @pl.when(first)
            def _():
                finish(1)

        else:
            down(1 + i, 0, 1)

    def own_step(k, carry):
        @pl.when(k >= len(tail) - 1)
        def _():
            down(k + 2, 0, 1)

        finish(k)
        return carry

    lax.fori_loop(jnp.where(first, 2, 0), plain, own_step, 0)
    for i, n in enumerate(tail):
        k = plain + i
        if k + 2 < chunks:
            down(k + 2, 0, 1)
        finish(k, n)

    twin_copy.wait_send()
    for d, other in others:
        for copy in route_copies(d, other):
            copy.wait_send()
    for d in range(1, chips):
        for q in range(parts):
            tok_copy(d, q).wait_send()
            forward_copy(d, q).wait_send()

    def drain(k, carry):
        for j in range(chips):
            pair_copy(j, k).wait_send()

        return carry

    lax.fori_loop(0, chunks, drain, 0)

    def drain_far(k, bits):
        for p in bits:
            for j in range(1, chips):
                back_copy(j, k, p).wait_send()

            @pl.when(now < steps - 1)
            def _():
                rise_copy(k, p).wait_send()

    def drain_one(k, carry):
        drain_far(k, whole)
        return carry

    lax.fori_loop(0, plain, drain_one, 0)
    for i, n in enumerate(tail):
        drain_far(plain + i, n)


def shards(mesh, tokens, route_ids, route_probs, step_size, start_state, w_gate, w_up, w_down):
    toks, width = tokens.shape[1:]
    topk = route_ids.shape[2]
    local, _, ff = w_gate.shape
    group = mesh.shape["expert"]
    steps = mesh.shape["tm"]
    chips = group // 2
    cap = 3 * toks * topk // (2 * local * group)
    slots = -(-2 * cap // 16) * 16
    dc = fit(width, DC)
    chunks = width // dc
    cuts = tuple(width * q // 16 for q in CUTS)

    smem = pl.BlockSpec(memory_space=pltpu.SMEM)
    hbm = pl.BlockSpec(memory_space=pl.ANY)
    dma = pltpu.SemaphoreType.DMA
    total = pl.pallas_call(
        functools.partial(kernel, (chips, steps, cap, slots, cuts, dc)),
        out_shape=pltpu.MemorySpace.VMEM((toks, width), F32),
        in_specs=[hbm, hbm, hbm, smem, hbm, hbm, hbm, hbm],
        out_specs=pl.BlockSpec(memory_space=pltpu.VMEM),
        scratch_shapes=[
            pltpu.VMEM((local, width, ff), BF16),
            pltpu.VMEM((local, width, ff), BF16),
            pltpu.VMEM((local, ff, width), BF16),
            pltpu.VMEM((toks, width), BF16),
            pltpu.VMEM((chips, 2 * toks, width), BF16),
            pltpu.VMEM((chips, 2, topk, 1, toks), jnp.int32),
            pltpu.VMEM((chips, 2, topk, 1, toks), F32),
            pltpu.VMEM((toks, width), F32),
            pltpu.VMEM((chips, local, slots, 128), F32),
            pltpu.VMEM((chips, local * slots, width), BF16),
            pltpu.VMEM((chips - 1, local, slots, ff), F32),
            pltpu.VMEM((chips - 1, local, slots, ff), F32),
            pltpu.VMEM((chips, local, slots, ff), BF16),
            pltpu.VMEM((chips, local * slots, 2 * toks), BF16),
            pltpu.VMEM((local * slots, dc), BF16),
            pltpu.VMEM((chips, chunks, toks, dc), F32),
            pltpu.VMEM((chips, chunks, toks, dc), BF16),
            pltpu.VMEM((chips, chunks, toks, dc), BF16),
            pltpu.VMEM((chips, chunks, toks, dc), BF16),
            pltpu.VMEM((chips, chunks, toks, dc), BF16),
            pltpu.VMEM((chunks, toks, dc), BF16),
            pltpu.VMEM((chunks, toks, dc), BF16),
            dma((4,)),
            dma((2, local)),
            dma((local,)),
            dma((chips - 1, PARTS)),
            dma((chips - 1, PARTS)),
            dma((chips - 1, 2, PARTS)),
            dma((1,)),
            dma((1,)),
            dma((chips, 2)),
            dma((chips, 2)),
            dma((chips, 2)),
            dma((chips, 2)),
            dma((chips, chunks)),
            dma((chips, chunks)),
            dma((chips - 1, chunks + SPARE)),
            dma((chips - 1, chunks + SPARE)),
            dma((chunks + SPARE,)),
            dma((chunks + SPARE,)),
            pltpu.SemaphoreType.REGULAR,
        ],
        compiler_params=pltpu.CompilerParams(
            collective_id=0, has_side_effects=True, vmem_limit_bytes=65_900_000
        ),
    )(
        tokens[0], jnp.transpose(route_ids, (2, 0, 1)), jnp.transpose(route_probs, (2, 0, 1)),
        step_size, start_state, w_gate, w_up, w_down,
    )
    return total[None]


def solution(mesh):
    return jax.shard_map(
        functools.partial(shards, mesh),
        mesh=mesh,
        in_specs=(
            P("tm", ("copies", "expert"), None),
            P("tm", ("copies", "expert"), None),
            P("tm", ("copies", "expert"), None),
            P(("copies", "tm")),
            P(("copies", "expert"), None),
            P("expert", None, None),
            P("expert", None, None),
            P("expert", None, None),
        ),
        out_specs=P("tm", ("copies", "expert"), None),
        check_vma=False,
    )
```
